32 devices in a mesh: groups: 2 (over x), seq: 8 (over z, y), head: 2 (over core).
Axes of the slice: x: 2, y: 2, z: 4, core: 2. Of those that a mesh axis runs over, the one named last changes fastest.
Arguments:
- query_proj: bfloat16 [4096, 2048], P(('groups', 'seq'), 'head'), parts along dimension 0, may hold values from -6 to 6
- key_proj: bfloat16 [4096, 2048], P(('groups', 'seq'), 'head'), parts along dimension 0, may hold values from -6 to 6
- value_proj: bfloat16 [4096, 2048], P(('groups', 'seq'), 'head'), parts along dimension 0, may hold values from -6 to 6
- segment_ids: int32 [4096], P(('groups', 'seq')), parts along dimension 0, may hold values from 0 to 5, never falling along the last dimension, each value on 1 to 682 neighbouring positions
- feature_map: bfloat16 [16, 128, 256], P('head'), may hold values from -0.5 to 0.5
- head_gain: float32 [2048], P('head'), may hold values from 0.1 to 1.9
- residual: bfloat16 [4096, 2048], P(('groups', 'seq', 'head')), parts along dimension 0, may hold values from -6 to 6
- out_weight: bfloat16 [2048, 2048], P('head'), may hold values from -0.125 to 0.125
- norm_gain: float32 [2048], replicated, may hold values from 0.1 to 1.9
- router: bfloat16 [2048, 16], replicated, may hold values from -0.125 to 0.125
- w_gate: bfloat16 [16, 2048, 1024], P(('seq', 'head')), may hold values from -0.125 to 0.125
- w_up: bfloat16 [16, 2048, 1024], P(('seq', 'head')), may hold values from -0.125 to 0.125
- w_down: bfloat16 [16, 1024, 2048], P(('seq', 'head')), may hold values from -0.1875 to 0.1875
- expert_ids: int32 [4096, 8], P(('groups', 'seq', 'head')), parts along dimension 0, may hold values from 0 to 15, all different within a row; in each aligned block of 128 rows (0 to 127, 128 to 255, ...) at most 80 rows name the same one
Outputs:
- hidden: bfloat16 [4096, 2048], P(('groups', 'seq', 'head')), parts along dimension 0
- expert_sum: bfloat16 [4096, 2048], P(('groups', 'seq', 'head')), parts along dimension 0
The draws below stay inside these ranges and needn't reach their ends.
There are 2 independent parts, one for each index of `groups`. The reference program is written for one: setup_inputs(seed, part) draws one part's arguments, and reference() takes and returns one part's arrays. A program takes and returns all parts, laid end to end along the dimension named above; an argument that names none is the same for every part. Nothing has to cross between parts.
Inputs may be any that keep to these rules, and one draw needn't show every extreme that they name: `segment_ids`: segment ids never fall; every segment has 1 to 682 tokens, one exactly 682. `expert_ids`: A token's 8 experts differ. In the 128 rows of one device (aligned blocks of rows) no expert is named more than 80 times, and in some such block some expert is named exactly 80 times.
All inputs are finite; a program needn't handle non-finite values.
Results may differ from the reference program's by a relative error of at most 0.011.
Values may be sent and summed in bfloat16 or wider, within the bound.
A program may use at most 128 MiB of HBM per device.

```python
import math
import jax
import jax.numpy as jnp
import numpy as np
from jax import lax

D = 2048
HEADS = 16
HD = 128
FEAT = 256
FF_E = 1024
TOPK = 8
SEG_COUNT = 6
TOK_DEV = 256
TOKENS = 2048
ROWS_DEV = 128
EXPERTS = 16
CAP = 80
SEG_MOST = 682
N_SEQ = 8


def block_scale(own_key, shape, shards, low, largest):
    level = 1.0
    for dim, blocks in shards:
        heights = jax.random.uniform(jax.random.fold_in(jax.random.fold_in(own_key, 6), dim), (blocks,), jnp.float32, low / len(shards), largest / len(shards))
        level = level * jnp.repeat(jnp.exp(heights), shape[dim] // blocks).reshape((-1,) + (1,) * (len(shape) - 1 - dim))
    return level


def length_profile(count, total, limit, lean):
    loads = [(1 << 20) // math.isqrt(standing ** lean) + 1 for standing in range(2, count + 1)]
    spare, holding = total - limit - (count - 1), [1] * (count - 1)
    while spare > 0:
        movable = [i for i in range(count - 1) if holding[i] < limit]
        whole, budget = sum([loads[i] for i in movable]), spare
        for i in movable:
            extra = min(limit - holding[i], max(1, budget * loads[i] // whole), spare)
            holding[i] = holding[i] + extra
            spare = spare - extra
    return np.array([limit] + holding)


def uneven(stream_key, number_of, total, most, slope):
    if number_of == 2:
        one = jax.random.randint(stream_key, (), max(1, total - most), min(most, total - 1) + 1)
        return jnp.stack([one, total - one])
    tallies = jnp.asarray(length_profile(number_of, total, most, slope), jnp.int32)
    twos = (number_of - 1) // 2
    source_of, taker = tallies[1:1 + 2 * twos:2], tallies[2:2 + 2 * twos:2]
    margin = jnp.minimum(source_of - 1, most - taker)
    shifted = jax.random.randint(jax.random.fold_in(stream_key, 1), (twos,), 0, 1 << 20) % (margin + 1)
    tallies = tallies.at[1:1 + 2 * twos:2].set(source_of - shifted).at[2:2 + 2 * twos:2].set(taker + shifted)
    return tallies[jax.random.permutation(jax.random.fold_in(stream_key, 2), number_of)]


def shared_out(stream_key, own, number, rows, number_of, top, reach, slope):
    ranking = jax.random.permutation(stream_key, number_of)
    crowded, common = portions_of(number_of, rows * top, reach, slope, True), portions_of(number_of, rows * top, reach, slope, False)
    places = jnp.arange(number_of)

    def named(tallies, offset_by):
        used = int((tallies > 0).sum())
        fixed = max(1, used // 4)
        passed = fixed + (places - fixed + offset_by * (used - fixed)) % max(1, number_of - fixed)
        return jnp.zeros((number_of,), jnp.int32).at[ranking[jnp.where(places < fixed, places, passed)]].set(jnp.asarray(tallies, jnp.int32))

    tallies = jnp.where(number % 4 == 0, named(crowded, number // 4), named(common, number - number // 4 - 1))
    mixed = jax.random.permutation(jax.random.fold_in(own, 3), number_of)
    donor, receiver = mixed[0:number_of // 2 * 2:2], mixed[1:number_of // 2 * 2:2]
    margin = jnp.minimum(tallies[donor] - 1, reach - tallies[receiver]) // 2
    margin = jnp.where((donor == ranking[0]) | (receiver == ranking[0]) | (tallies[receiver] == 0), 0, jnp.maximum(margin, 0))
    passed = jax.random.randint(jax.random.fold_in(own, 4), (number_of // 2,), 0, 1 << 20) % (margin + 1)
    tallies = tallies.at[donor].add(-passed).at[receiver].add(passed)
    members = jnp.searchsorted(jnp.cumsum(tallies), jnp.arange(rows * top), side="right").astype(jnp.int32)
    table = members.reshape(top, rows).T
    table = table[jax.random.permutation(jax.random.fold_in(own, 1), rows)]
    offset_by = jax.random.randint(jax.random.fold_in(own, 2), (rows, 1), 0, top)
    return jnp.take_along_axis(table, (jnp.arange(top)[None, :] + offset_by) % top, axis=1)


def portions_of(number_of, total, bound, lean, full):
    weights = [(1 << 20) // math.isqrt(rank ** lean) + 1 for rank in range(1, number_of + 1)]
    largest = bound if full else min(bound, max(-(-total // number_of), total * weights[0] // sum(weights)))
    least = 1 if total - largest >= number_of - 1 else 0
    counts, rest = [largest] + [least] * (number_of - 1), total - largest - least * (number_of - 1)
    while rest > 0:
        movable = [i for i in range(1, number_of) if counts[i] < largest] or [i for i in range(1, number_of) if counts[i] < bound]
        mass, left = sum([weights[i] for i in movable]), rest
        for i in movable:
            extra = min(bound - counts[i], max(1, left * weights[i] // mass), rest)
            counts[i] = counts[i] + extra
            rest = rest - extra
    return np.array(counts)


def bell_draw(stream_key, extent, scale, limit, cuts=(), held_as=jnp.bfloat16):
    level = block_scale(stream_key, extent, cuts, -0.22, 0.18) if cuts else 1.0
    result = jax.random.normal(stream_key, extent, jnp.float32) * scale * level
    return jnp.minimum(jnp.maximum(result, -limit), limit).astype(held_as)


def setup_inputs(seed: int = 0, part: int = 0) -> dict:
    streams_of = jax.random.split(jax.random.key(seed), 15)
    own_keys = jax.random.split(jax.random.fold_in(streams_of[14], part), 15)
    query_proj = bell_draw(own_keys[0], (TOKENS, D), 1.0, 6.0, ((0, 8), (1, 2)))
    key_proj = bell_draw(own_keys[1], (TOKENS, D), 1.0, 6.0, ((0, 8), (1, 2)))
    value_proj = bell_draw(own_keys[2], (TOKENS, D), 1.0, 6.0, ((0, 8), (1, 2)))
    segment_ids = jnp.searchsorted(jnp.cumsum(uneven(own_keys[3], SEG_COUNT, TOKENS, SEG_MOST, 1)), jnp.arange(TOKENS), side="right").astype(jnp.int32)
    feature_map = bell_draw(streams_of[4], (HEADS, HD, FEAT), HD ** -0.5, 0.5, ((0, 2),))
    head_gain = jnp.clip(1.0 + 0.18 * jax.random.normal(streams_of[5], (D,), jnp.float32), 0.1, 1.9)
    residual = bell_draw(own_keys[6], (TOKENS, D), 1.0, 6.0, ((0, 16),))
    out_weight = bell_draw(streams_of[7], (D, D), D ** -0.5, 0.125, ((0, 2),))
    norm_gain = jnp.clip(1.0 + 0.18 * jax.random.normal(streams_of[8], (D,), jnp.float32), 0.1, 1.9)
    router = bell_draw(streams_of[9], (D, EXPERTS), D ** -0.5, 0.125)
    w_gate = bell_draw(streams_of[10], (EXPERTS, D, FF_E), D ** -0.5, 0.125, ((0, 16),))
    w_up = bell_draw(streams_of[11], (EXPERTS, D, FF_E), D ** -0.5, 0.125, ((0, 16),))
    w_down = bell_draw(streams_of[12], (EXPERTS, FF_E, D), FF_E ** -0.5, 0.1875, ((0, 16),))
    expert_ids_keys = jax.random.split(jax.random.fold_in(own_keys[13], 1), TOKENS // ROWS_DEV)
    expert_ids_turns = jax.random.permutation(jax.random.fold_in(own_keys[13], 3), TOKENS // ROWS_DEV)
    expert_ids = jax.vmap(lambda own, number: shared_out(jax.random.fold_in(own_keys[13], 2), own, number, ROWS_DEV, EXPERTS, TOPK, CAP, 2))(expert_ids_keys, expert_ids_turns).reshape((TOKENS, TOPK))
    return dict(query_proj=query_proj, key_proj=key_proj, value_proj=value_proj, segment_ids=segment_ids, feature_map=feature_map, head_gain=head_gain, residual=residual, out_weight=out_weight, norm_gain=norm_gain, router=router, w_gate=w_gate, w_up=w_up, w_down=w_down, expert_ids=expert_ids)


def features_of(block, feature_map):
    grouped = block.reshape(TOK_DEV, HEADS, HD).astype(jnp.float32)
    projected = jnp.einsum('thd,hdf->thf', grouped, feature_map.astype(jnp.float32), precision=lax.Precision.HIGHEST)
    rounded = lax.optimization_barrier((jax.nn.elu(projected) + 1.0).astype(jnp.bfloat16))
    return rounded.astype(jnp.float32)

def reference(query_proj, key_proj, value_proj, segment_ids, feature_map, head_gain, residual, out_weight, norm_gain, router, w_gate, w_up, w_down, expert_ids):
    highest = lax.Precision.HIGHEST
    positions = jnp.arange(TOK_DEV, dtype=jnp.int32)
    causal = positions[None, :] <= positions[:, None]

    def block_step(carry, operands):
        seg_prev, state_prev = carry
        query_block, key_block, value_block, seg_block = operands
        query_feat = features_of(query_block, feature_map)
        key_feat = features_of(key_block, feature_map)
        values = value_block.reshape(TOK_DEV, HEADS, HD).astype(jnp.float32)
        scores = jnp.einsum('thf,shf->hts', query_feat, key_feat, precision=highest)
        allowed = causal & (seg_block[None, :] == seg_block[:, None])
        weights_b = lax.optimization_barrier(jnp.where(allowed[None], scores, 0.0).astype(jnp.bfloat16))
        within = jnp.einsum('hts,shd->thd', weights_b.astype(jnp.float32), values, precision=highest)
        carried = jnp.einsum('thf,hfd->thd', query_feat, state_prev, precision=highest)
        carry_mask = (seg_block == seg_prev).astype(jnp.float32)
        mixed = within + carry_mask[:, None, None] * carried
        last_seg = seg_block[TOK_DEV - 1]
        tail_mask = (seg_block == last_seg).astype(jnp.float32)
        local_state = jnp.einsum('thf,thd->hfd', key_feat * tail_mask[:, None, None], values, precision=highest)
        same_seg = (seg_prev == last_seg).astype(jnp.float32)
        new_state = local_state + same_seg * state_prev
        scale = lax.rsqrt(lax.optimization_barrier(jnp.mean(mixed * mixed, axis=2, keepdims=True)) + 1e-06)
        attn_block = (mixed * scale * head_gain.reshape(HEADS, HD)).reshape(TOK_DEV, D).astype(jnp.bfloat16)
        return ((last_seg, new_state), attn_block)
    init = (jnp.array(-1, dtype=jnp.int32), jnp.zeros((HEADS, FEAT, HD), jnp.float32))
    operands = (query_proj.reshape(N_SEQ, TOK_DEV, D), key_proj.reshape(N_SEQ, TOK_DEV, D), value_proj.reshape(N_SEQ, TOK_DEV, D), segment_ids.reshape(N_SEQ, TOK_DEV))
    final_carry, attn_blocks = lax.scan(block_step, init, operands)
    attn = attn_blocks.reshape(TOKENS, D)
    projected = jnp.dot(attn, out_weight, preferred_element_type=jnp.float32)
    hidden = (residual.astype(jnp.float32) + projected).astype(jnp.bfloat16)
    hidden_f = hidden.astype(jnp.float32)
    normed = (hidden_f * lax.rsqrt(lax.optimization_barrier(jnp.mean(hidden_f * hidden_f, axis=1, keepdims=True)) + 1e-05) * norm_gain).astype(jnp.bfloat16)
    logits = jnp.dot(normed, router, preferred_element_type=jnp.float32)
    picked = expert_ids[:, :, None] == jnp.arange(EXPERTS, dtype=jnp.int32)[None, None, :]
    chosen = lax.optimization_barrier(jnp.sum(jnp.where(picked, logits[:, None, :], 0.0), axis=2))
    gates = jax.nn.sigmoid(chosen)
    gate_weights = gates / lax.optimization_barrier(jnp.sum(gates, axis=1, keepdims=True))
    block_count = TOKENS // ROWS_DEV
    flat_ids = expert_ids.reshape(block_count, ROWS_DEV * TOPK)
    onehot = (flat_ids[:, :, None] == jnp.arange(EXPERTS, dtype=jnp.int32)[None, None, :]).astype(jnp.int32)
    slots = lax.optimization_barrier(jnp.sum((jnp.cumsum(onehot, axis=1) - onehot) * onehot, axis=2))
    block_index = jnp.arange(block_count, dtype=jnp.int32)[:, None]
    targets = (flat_ids * (block_count * CAP) + block_index * CAP + slots).reshape(-1).astype(jnp.int32)
    row_of = (jnp.arange(TOKENS * TOPK, dtype=jnp.int32) // TOPK).astype(jnp.int32)
    table = jnp.full((EXPERTS * block_count * CAP,), TOKENS, dtype=jnp.int32).at[targets].set(row_of)
    padded = jnp.concatenate([normed, jnp.zeros((1, D), jnp.bfloat16)], axis=0)

    def run_expert(operands_e):
        indices, gate_e, up_e, down_e = operands_e
        rows_in = padded[indices]
        gate_pre = jnp.dot(rows_in, gate_e, preferred_element_type=jnp.float32)
        up_pre = jnp.dot(rows_in, up_e, preferred_element_type=jnp.float32)
        activated = (jax.nn.silu(gate_pre) * up_pre).astype(jnp.bfloat16)
        return jnp.dot(activated, down_e, preferred_element_type=jnp.float32).astype(jnp.bfloat16)
    results = lax.map(run_expert, (table.reshape(EXPERTS, block_count * CAP), w_gate, w_up, w_down))
    outputs = results.reshape(EXPERTS * block_count * CAP, D)[targets].reshape(TOKENS, TOPK, D)
    expert_sum = lax.optimization_barrier(jnp.sum(gate_weights[:, :, None] * outputs.astype(jnp.float32), axis=1)).astype(jnp.bfloat16)
    return (hidden, expert_sum)
```

```python
import jax
import jax.numpy as jnp
from jax import lax
from jax.sharding import PartitionSpec as P


def carried_in(last_seg, local_state, token_count):
    place = lax.axis_index("seq")
    blocks = lax.axis_size("seq")
    longest = token_count * blocks // 3
    reach = min(blocks - 1, max(1, (longest - 2) // token_count + 1))
    last_all = lax.all_gather(last_seg, "seq")

    def last_of(back):
        index = place - back
        return jnp.where(index >= 0, last_all[jnp.maximum(index, 0)], -1 - back)

    before = last_of(1)
    carried = None
    window = local_state
    span = 1
    covered = 0
    while covered < reach:
        shifted = lax.ppermute(
            window.astype(jnp.bfloat16), "seq", [(i, i + span) for i in range(blocks - span)]
        ).astype(jnp.float32)
        if carried is None:
            carried = shifted
        else:
            carried = carried + jnp.where(last_of(span) == before, shifted, 0.0)
        covered += span
        if covered < reach:
            window = window + jnp.where(last_of(span) == last_seg, shifted, 0.0)
        span *= 2
    return before, carried


def features_of(inputs, feature_map, head_count, head_dim):
    grouped = inputs.reshape(inputs.shape[0], head_count, head_dim)
    projected = jnp.einsum("thd,hdf->thf", grouped, feature_map, preferred_element_type=jnp.float32)
    return (jax.nn.elu(projected) + 1.0).astype(jnp.bfloat16)


def run_expert(rows, gate, w_gate, w_up, w_down):
    gate_pre = jnp.dot(rows, w_gate, preferred_element_type=jnp.float32)
    up_pre = jnp.dot(rows, w_up, preferred_element_type=jnp.float32)
    activated = (jax.nn.silu(gate_pre) * up_pre).astype(jnp.bfloat16)
    answer = jnp.dot(activated, w_down, preferred_element_type=jnp.float32)
    return answer * gate[:, None]


def shards(
    query_proj,
    key_proj,
    value_proj,
    segment_ids,
    feature_map,
    head_gain,
    residual,
    out_weight,
    norm_gain,
    router,
    w_gate,
    w_up,
    w_down,
    expert_ids,
):
    token_count = query_proj.shape[0]
    head_count = feature_map.shape[0]
    head_dim = feature_map.shape[1]
    query_feat = features_of(query_proj, feature_map, head_count, head_dim)
    key_feat = features_of(key_proj, feature_map, head_count, head_dim)
    values = value_proj.reshape(token_count, head_count, head_dim)
    last_seg = segment_ids[token_count - 1]
    tail_mask = (segment_ids == last_seg).astype(jnp.bfloat16)
    local_state = jnp.einsum(
        "thf,thd->hfd",
        key_feat * tail_mask[:, None, None],
        values,
        preferred_element_type=jnp.float32,
    )
    seg_before, state_before = carried_in(last_seg, local_state, token_count)
    scores = jnp.einsum("thf,shf->hts", query_feat, key_feat, preferred_element_type=jnp.float32)
    positions = lax.iota(jnp.int32, token_count)
    allowed = (positions[None, :] <= positions[:, None]) & (
        segment_ids[None, :] == segment_ids[:, None]
    )
    block_weights = jnp.where(allowed[None], scores, 0.0).astype(jnp.bfloat16)
    within = jnp.einsum("hts,shd->thd", block_weights, values, preferred_element_type=jnp.float32)
    carried = jnp.einsum(
        "thf,hfd->thd",
        query_feat,
        state_before.astype(jnp.bfloat16),
        preferred_element_type=jnp.float32,
    )
    carry_mask = (segment_ids == seg_before).astype(jnp.float32)
    mixed = within + carry_mask[:, None, None] * carried
    scale = lax.rsqrt(jnp.mean(mixed * mixed, axis=2, keepdims=True) + 1e-06)
    attn_heads = (
        (mixed * scale * head_gain.reshape(head_count, head_dim))
        .reshape(token_count, head_count * head_dim)
        .astype(jnp.bfloat16)
    )
    attn_rows = lax.all_to_all(attn_heads, "head", split_axis=0, concat_axis=1, tiled=True)
    projected = jnp.dot(
        attn_rows,
        lax.all_gather(out_weight, "head", axis=0, tiled=True),
        preferred_element_type=jnp.float32,
    )
    hidden = (residual.astype(jnp.float32) + projected).astype(jnp.bfloat16)
    hidden_f = hidden.astype(jnp.float32)
    normed = (
        hidden_f
        * lax.rsqrt(jnp.mean(hidden_f * hidden_f, axis=1, keepdims=True) + 1e-05)
        * norm_gain
    ).astype(jnp.bfloat16)
    logits = jnp.dot(normed, router, preferred_element_type=jnp.float32)
    expert_count = router.shape[1]
    expert_iota = lax.iota(jnp.int32, expert_count)
    picked = expert_ids[:, :, None] == expert_iota[None, None, :]
    chosen = jnp.sum(jnp.where(picked, logits[:, None, :], 0.0), axis=2)
    gates = jax.nn.sigmoid(chosen)
    gate_weights = gates / jnp.sum(gates, axis=1, keepdims=True)
    dense_gates = jnp.sum(jnp.where(picked, gate_weights[:, :, None], 0.0), axis=1)
    spread = ("seq", "head")
    all_rows = lax.all_gather(normed, spread, axis=0, tiled=True)
    all_gates = lax.all_gather(dense_gates, spread, axis=0, tiled=True)
    exp_dev = w_gate.shape[0]
    first = (lax.axis_index("seq") * lax.axis_size("head") + lax.axis_index("head")) * exp_dev
    partial = 0.0
    for own in range(exp_dev):
        gate = jnp.sum(jnp.where(expert_iota[None, :] == first + own, all_gates, 0.0), axis=1)
        partial = partial + run_expert(all_rows, gate, w_gate[own], w_up[own], w_down[own])
    expert_sum = lax.psum_scatter(
        partial.astype(jnp.bfloat16), spread, scatter_dimension=0, tiled=True
    )
    return (hidden, expert_sum)


def solution(mesh):
    placed = (
        P(("groups", "seq"), "head"),
        P(("groups", "seq"), "head"),
        P(("groups", "seq"), "head"),
        P(("groups", "seq")),
        P("head", None, None),
        P("head"),
        P(("groups", "seq", "head"), None),
        P("head", None),
        P(),
        P(),
        P(("seq", "head"), None, None),
        P(("seq", "head"), None, None),
        P(("seq", "head"), None, None),
        P(("groups", "seq", "head"), None),
    )
    return jax.shard_map(
        shards,
        mesh=mesh,
        in_specs=placed,
        out_specs=(P(("groups", "seq", "head"), None), P(("groups", "seq", "head"), None)),
        check_vma=False,
    )
```

```python
import functools

import jax
import jax.numpy as jnp
from jax import lax
from jax.experimental import pallas as pl
from jax.experimental.pallas import tpu as pltpu
from jax.sharding import PartitionSpec as P


def carried_in(last_seg, local_state, token_count):
    blocks = lax.axis_size("seq")
    longest = token_count * blocks // 3
    reach = min(blocks - 1, max(1, (longest - 2) // token_count + 1))
    state_rows = local_state.shape[0] * local_state.shape[1]
    width = local_state.shape[2]
    before = None
    carried = None
    window = local_state
    span = 1
    covered = 0
    while covered < reach:
        packet = jnp.concatenate(
            [
                window.reshape(state_rows, width).astype(jnp.bfloat16),
                jnp.full((16, width), last_seg, jnp.bfloat16),
            ]
        )
        arrived = lax.ppermute(packet, "seq", [(i, i + span) for i in range(blocks - span)])
        shifted = arrived[:state_rows].astype(jnp.float32).reshape(local_state.shape)
        seg = arrived[state_rows, 0].astype(jnp.int32)
        if carried is None:
            before, carried = seg, shifted
        else:
            carried = carried + jnp.where(seg == before, shifted, 0.0)
        covered += span
        if covered < reach:
            window = window + jnp.where(seg == last_seg, shifted, 0.0)
        span *= 2
    return before, carried


def features_of(inputs, feature_map, head_count, head_dim):
    grouped = inputs.reshape(inputs.shape[0], head_count, head_dim)
    projected = jnp.einsum("thd,hdf->thf", grouped, feature_map, preferred_element_type=jnp.float32)
    return (jax.nn.elu(projected) + 1.0).astype(jnp.bfloat16)


def run_expert(rows, gate, w_gate, w_up, w_down):
    gate_pre = jnp.dot(rows, w_gate, preferred_element_type=jnp.float32)
    up_pre = jnp.dot(rows, w_up, preferred_element_type=jnp.float32)
    activated = (jax.nn.silu(gate_pre) * up_pre).astype(jnp.bfloat16)
    answer = jnp.dot(activated, w_down, preferred_element_type=jnp.float32)
    return answer * gate[:, None]


MESH = pl.DeviceIdType.MESH
TILE = 256
VMEM_MOST = 63 * 1024 * 1024


def ring_place(index, count, folded):
    if not folded:
        return index
    far, side = index // 2, index % 2
    return far + side * (count - 1 - 2 * far)


def ring_index(place, count, folded):
    if not folded:
        return place
    side = place // (count // 2)
    far = place + side * (count - 1 - 2 * place)
    return 2 * far + side


def moe_kernel(
    count,
    folded,
    experts,
    x_ref,
    wg_hbm,
    wu_hbm,
    wd_hbm,
    out_ref,
    rows_buf,
    part,
    pair,
    inbox,
    wg,
    wu,
    wd,
    act,
    load_sem,
    ag_send,
    ag_recv,
    sib_send,
    sib_recv,
    rs_send,
    rs_recv,
    pair_send,
    pair_recv,
):
    rows, padded = x_ref.shape
    width = out_ref.shape[1]
    half = rows // 2
    far = count // 2
    core = lax.axis_index("head")
    seq = lax.axis_index("seq")
    place = ring_place(seq, count, folded)
    ahead = {"seq": ring_index((place + 1) % count, count, folded)}
    behind = {"seq": ring_index((place + count - 1) % count, count, folded)}
    sibling = {"head": 1 - core}
    toward = (ahead, behind)

    loads = [
        pltpu.make_async_copy(src.at[0], dst, load_sem.at[i])
        for i, (src, dst) in enumerate(((wg_hbm, wg), (wu_hbm, wu), (wd_hbm, wd)))
    ]
    for load in loads:
        load.start()

    barrier = pltpu.get_barrier_semaphore()
    for other in (ahead, behind, sibling):
        pl.semaphore_signal(barrier, inc=1, device_id=other, device_id_type=MESH)
    pl.semaphore_wait(barrier, 3)

    def spot(slot):
        if slot == 0:
            return 0
        if slot == far:
            return count - 1
        return 2 * slot - 1 if slot < far else 2 * (count - slot)

    def start_row(slot, which, part_of=0):
        return pl.multiple_of((spot(slot) * 2 + which) * rows + part_of * half, half)

    def block(ref, slot, which):
        return ref.at[pl.ds(start_row(slot, which), rows)]

    def chunk(ref, slot, which, h):
        return ref.at[pl.ds(start_row(slot, which, h), half)]

    def slot_of(way, hop):
        return hop if way == 0 else (count - hop) % count

    own_copy = pltpu.make_async_copy(x_ref, block(rows_buf, 0, core), load_sem.at[3])
    own_copy.start()

    gathers = {}
    for way in range(2):
        for hop in range(far):
            for h in range(2):
                if hop == far - 1 and h != way:
                    continue
                if hop == 0:
                    src = x_ref.at[pl.ds(h * half, half)]
                else:
                    src = chunk(rows_buf, slot_of(way, hop), core, h)
                gathers[way, hop, h] = pltpu.make_async_remote_copy(
                    src_ref=src,
                    dst_ref=chunk(rows_buf, slot_of(way, hop + 1), core, h),
                    send_sem=ag_send.at[way, hop, h],
                    recv_sem=ag_recv.at[way, hop, h],
                    device_id=toward[way],
                    device_id_type=MESH,
                )

    shares = {}
    answers = {}
    for slot in range(count):
        src = x_ref if slot == 0 else block(rows_buf, slot, core)
        shares[slot] = pltpu.make_async_remote_copy(
            src_ref=src,
            dst_ref=block(rows_buf, slot, core),
            send_sem=sib_send.at[slot],
            recv_sem=sib_recv.at[slot],
            device_id=sibling,
            device_id_type=MESH,
        )
        answers[slot] = pltpu.make_async_remote_copy(
            src_ref=block(part, slot, 1 - core),
            dst_ref=pair.at[slot],
            send_sem=pair_send.at[slot],
            recv_sem=pair_recv.at[slot],
            device_id=sibling,
            device_id_type=MESH,
        )

    def compute(first_slot, blocks):
        low = spot(first_slot) * 2 * rows
        tall = blocks * 2 * rows
        expert = lax.axis_index("seq") * 2 + core
        taken = pl.ds(low, tall)
        extra = rows_buf[taken, width:].astype(jnp.float32)
        lane = lax.broadcasted_iota(jnp.int32, extra.shape, 1)
        mine = (lane == expert) | (lane == expert + experts)
        gate = jnp.sum(jnp.where(mine, extra, 0.0), axis=1, keepdims=True)

        def up_step(t, carry):
            cols = pl.ds(pl.multiple_of(t * TILE, TILE), TILE)
            x = rows_buf[taken, :width]
            gate_pre = jnp.dot(x, wg[:, cols], preferred_element_type=jnp.float32)
            up_pre = jnp.dot(x, wu[:, cols], preferred_element_type=jnp.float32)
            act[:tall, cols] = (gate_pre * jax.nn.sigmoid(gate_pre) * up_pre).astype(jnp.bfloat16)
            return carry

        lax.fori_loop(0, wg.shape[1] // TILE, up_step, 0)

        def down_step(t, carry):
            cols = pl.ds(pl.multiple_of(t * TILE, TILE), TILE)
            answer = jnp.dot(act[:tall, :], wd[:, cols], preferred_element_type=jnp.float32)
            part[taken, cols] = (answer * gate).astype(jnp.bfloat16)
            return carry

        lax.fori_loop(0, width // TILE, down_step, 0)

    sums = {}
    for way in range(2):
        for hop in range(far, 0, -1):
            for h in range(2):
                if hop == far and h != way:
                    continue
                sums[way, hop, h] = pltpu.make_async_remote_copy(
                    src_ref=chunk(part, slot_of(way, hop), core, h),
                    dst_ref=inbox.at[way, hop - 1, h],
                    send_sem=rs_send.at[way, hop - 1, h],
                    recv_sem=rs_recv.at[way, hop - 1, h],
                    device_id=toward[1 - way],
                    device_id_type=MESH,
                )

    def add_and_send(way, hop, h):
        slot = slot_of(way, hop)
        here = pl.ds(start_row(slot, core, h), half)
        total = part[here, :].astype(jnp.float32) + pair[slot, h * half : (h + 1) * half, :].astype(
            jnp.float32
        )
        if (way, hop + 1, h) in sums:
            sums[way, hop + 1, h].wait_recv()
            total = total + inbox[way, hop, h].astype(jnp.float32)
        part[here, :] = total.astype(jnp.bfloat16)
        sums[way, hop, h].start()

    for h in range(2):
        for way in range(2):
            at = h if way == 0 else 1 - h
            if (way, 0, at) in gathers:
                gathers[way, 0, at].start()
    shares[0].start()
    for load in loads:
        load.wait()
    own_copy.wait()
    shares[0].wait_recv()
    compute(0, 1)
    answers[0].start()
    for hop in range(1, far + 1):
        for h in range(2):
            for way in range(2):
                at = h if way == 0 else 1 - h
                if (way, hop - 1, at) in gathers:
                    gathers[way, hop - 1, at].wait_recv()
                if (way, hop, at) in gathers:
                    gathers[way, hop, at].start()
        slots = (hop, count - hop) if hop < far else (far,)
        for slot in slots:
            shares[slot].start()
        for slot in slots:
            shares[slot].wait_recv()
        compute(hop, len(slots))
        for slot in slots:
            answers[slot].start()
        if hop == far - 1:
            for way in range(2):
                answers[slot_of(way, hop)].wait_recv()
            for way in range(2):
                add_and_send(way, hop, 1 - way)

    answers[far].wait_recv()
    for way in range(2):
        add_and_send(way, far, way)
    for way in range(2):
        add_and_send(way, far - 1, way)
    for hop in range(far - 2, 0, -1):
        for way in range(2):
            answers[slot_of(way, hop)].wait_recv()
        for turn in range(2):
            for way in range(2):
                add_and_send(way, hop, 1 - way if turn == 0 else way)
    answers[0].wait_recv()
    for h in range(2):
        here = pl.ds(start_row(0, core, h), half)
        total = part[here, :].astype(jnp.float32) + pair[0, h * half : (h + 1) * half, :].astype(
            jnp.float32
        )
        for way in range(2):
            if (way, 1, h) in sums:
                sums[way, 1, h].wait_recv()
                total = total + inbox[way, 0, h].astype(jnp.float32)
        out_ref[h * half : (h + 1) * half, :] = total.astype(out_ref.dtype)
    for group in (gathers, shares, answers, sums):
        for copy in group.values():
            copy.wait_send()


def moe_scratch(count, rows, padded, width, hidden):
    half = rows // 2
    far = count // 2
    tall = count * 2 * rows
    bf16 = jnp.bfloat16
    return [
        ((tall, padded), bf16),
        ((tall, width), bf16),
        ((count, rows, width), bf16),
        ((2, far, 2, half, width), bf16),
        ((width, hidden), bf16),
        ((width, hidden), bf16),
        ((hidden, width), bf16),
        ((4 * rows, hidden), bf16),
    ]


def moe(rows_in, width, experts, w_gate, w_up, w_down, folded):
    count = lax.axis_size("seq")
    rows, padded = rows_in.shape
    far = count // 2
    dma = pltpu.SemaphoreType.DMA
    scratch = moe_scratch(count, rows, padded, width, w_gate.shape[2])
    tall = count * 2 * rows
    return pl.pallas_call(
        functools.partial(moe_kernel, count, folded, experts),
        out_shape=jax.ShapeDtypeStruct((rows, width), jnp.bfloat16),
        in_specs=[pl.BlockSpec(memory_space=pltpu.VMEM)]
        + [pl.BlockSpec(memory_space=pl.ANY)] * 3,
        out_specs=pl.BlockSpec(memory_space=pltpu.VMEM),
        scratch_shapes=[pltpu.VMEM(shape, dtype) for shape, dtype in scratch]
        + [
            dma((4,)),
            dma((2, far, 2)),
            dma((2, far, 2)),
            dma((count,)),
            dma((count,)),
            dma((2, far, 2)),
            dma((2, far, 2)),
            dma((count,)),
            dma((count,)),
        ],
        compiler_params=pltpu.CompilerParams(
            collective_id=0, has_side_effects=True, vmem_limit_bytes=VMEM_MOST
        ),
        cost_estimate=pl.CostEstimate(
            flops=6 * tall * width * w_gate.shape[2],
            bytes_accessed=6 * width * w_gate.shape[2],
            transcendentals=tall * w_gate.shape[2],
        ),
    )(rows_in, w_gate, w_up, w_down)


def moe_fits(count, heads, rows, padded, width, w_gate):
    if heads != 2 or count < 4 or count % 2 or w_gate.shape[0] != 1:
        return False
    if rows % 32 or width % TILE or w_gate.shape[2] % TILE:
        return False
    need = 0
    for shape, _ in moe_scratch(count, rows, padded, width, w_gate.shape[2]):
        size = 2
        for extent in shape:
            size *= extent
        need += size
    return need < VMEM_MOST * 7 // 8


def shards(
    folded,
    query_proj,
    key_proj,
    value_proj,
    segment_ids,
    feature_map,
    head_gain,
    residual,
    out_weight,
    norm_gain,
    router,
    w_gate,
    w_up,
    w_down,
    expert_ids,
):
    token_count = query_proj.shape[0]
    head_count = feature_map.shape[0]
    head_dim = feature_map.shape[1]
    query_feat = features_of(query_proj, feature_map, head_count, head_dim)
    key_feat = features_of(key_proj, feature_map, head_count, head_dim)
    values = value_proj.reshape(token_count, head_count, head_dim)
    last_seg = segment_ids[token_count - 1]
    tail_mask = (segment_ids == last_seg).astype(jnp.bfloat16)
    local_state = jnp.einsum(
        "thf,thd->hfd",
        key_feat * tail_mask[:, None, None],
        values,
        preferred_element_type=jnp.float32,
    )
    seg_before, state_before = carried_in(last_seg, local_state, token_count)
    scores = jnp.einsum("thf,shf->hts", query_feat, key_feat, preferred_element_type=jnp.float32)
    positions = lax.iota(jnp.int32, token_count)
    allowed = (positions[None, :] <= positions[:, None]) & (
        segment_ids[None, :] == segment_ids[:, None]
    )
    block_weights = jnp.where(allowed[None], scores, 0.0).astype(jnp.bfloat16)
    within = jnp.einsum("hts,shd->thd", block_weights, values, preferred_element_type=jnp.float32)
    carried = jnp.einsum(
        "thf,hfd->thd",
        query_feat,
        state_before.astype(jnp.bfloat16),
        preferred_element_type=jnp.float32,
    )
    carry_mask = (segment_ids == seg_before).astype(jnp.float32)
    mixed = within + carry_mask[:, None, None] * carried
    scale = lax.rsqrt(jnp.mean(mixed * mixed, axis=2, keepdims=True) + 1e-06)
    attn_heads = (
        (mixed * scale * head_gain.reshape(head_count, head_dim))
        .reshape(token_count, head_count * head_dim)
        .astype(jnp.bfloat16)
    )
    row_count = residual.shape[0]
    head_place = lax.axis_index("head")
    head_devs = lax.axis_size("head")
    sums = jnp.dot(attn_heads, out_weight, preferred_element_type=jnp.float32)
    projected = lax.dynamic_slice_in_dim(sums, head_place * row_count, row_count)
    for step in range(1, head_devs):
        target = (head_place + step) % head_devs
        projected = projected + lax.ppermute(
            lax.dynamic_slice_in_dim(sums, target * row_count, row_count),
            "head",
            [(i, (i + step) % head_devs) for i in range(head_devs)],
        )
    hidden = (residual.astype(jnp.float32) + projected).astype(jnp.bfloat16)
    hidden_f = hidden.astype(jnp.float32)
    normed = (
        hidden_f
        * lax.rsqrt(jnp.mean(hidden_f * hidden_f, axis=1, keepdims=True) + 1e-05)
        * norm_gain
    ).astype(jnp.bfloat16)
    logits = jnp.dot(normed, router, preferred_element_type=jnp.float32)
    expert_count = router.shape[1]
    expert_iota = lax.iota(jnp.int32, expert_count)
    picked = expert_ids[:, :, None] == expert_iota[None, None, :]
    chosen = jnp.sum(jnp.where(picked, logits[:, None, :], 0.0), axis=2)
    gates = jax.nn.sigmoid(chosen)
    gate_weights = gates / jnp.sum(gates, axis=1, keepdims=True)
    dense_gates = jnp.sum(jnp.where(picked, gate_weights[:, :, None], 0.0), axis=1)
    model_width = normed.shape[1]
    coarse = lax.reduce_precision(dense_gates, 8, 7)
    lanes = -(-2 * expert_count // 128) * 128
    extra = jnp.concatenate([coarse, dense_gates - coarse], axis=1).astype(jnp.bfloat16)
    extra = jnp.pad(extra, ((0, 0), (0, lanes - 2 * expert_count)))
    if moe_fits(lax.axis_size("seq"), head_devs, row_count, model_width + lanes, model_width, w_gate):
        rows_in = jnp.concatenate([normed, extra], axis=1)
        expert_sum = moe(rows_in, model_width, expert_count, w_gate, w_up, w_down, folded)
        return (hidden, expert_sum)
    spread = ("seq", "head")
    all_rows = lax.all_gather(normed, spread, axis=0, tiled=True)
    all_gates = lax.all_gather(dense_gates, spread, axis=0, tiled=True)
    exp_dev = w_gate.shape[0]
    first = (lax.axis_index("seq") * lax.axis_size("head") + lax.axis_index("head")) * exp_dev
    partial = 0.0
    for own in range(exp_dev):
        gate = jnp.sum(jnp.where(expert_iota[None, :] == first + own, all_gates, 0.0), axis=1)
        partial = partial + run_expert(all_rows, gate, w_gate[own], w_up[own], w_down[own])
    expert_sum = lax.psum_scatter(
        partial.astype(jnp.bfloat16), spread, scatter_dimension=0, tiled=True
    )
    return (hidden, expert_sum)


def folded_seq(mesh):
    chips = [getattr(d, "coords", None) for d in mesh.devices[0, :3, 0]]
    if None in chips or len(chips) < 3:
        return True
    moved = [sum(abs(i - j) for i, j in zip(a, b)) for a, b in zip(chips, chips[1:])]
    return moved[0] == 1 and moved[1] == 2


def solution(mesh):
    placed = (
        P(("groups", "seq"), "head"),
        P(("groups", "seq"), "head"),
        P(("groups", "seq"), "head"),
        P(("groups", "seq")),
        P("head", None, None),
        P("head"),
        P(("groups", "seq", "head"), None),
        P("head", None),
        P(),
        P(),
        P(("seq", "head"), None, None),
        P(("seq", "head"), None, None),
        P(("seq", "head"), None, None),
        P(("groups", "seq", "head"), None),
    )
    return jax.shard_map(
        functools.partial(shards, folded_seq(mesh)),
        mesh=mesh,
        in_specs=placed,
        out_specs=(P(("groups", "seq", "head"), None), P(("groups", "seq", "head"), None)),
        check_vma=False,
    )
```

```python
import functools

import jax
import jax.numpy as jnp
from jax import lax
from jax.experimental import pallas as pl
from jax.experimental.pallas import tpu as pltpu
from jax.sharding import PartitionSpec as P


def run_expert(rows, gate, w_gate, w_up, w_down):
    gate_pre = jnp.dot(rows, w_gate, preferred_element_type=jnp.float32)
    up_pre = jnp.dot(rows, w_up, preferred_element_type=jnp.float32)
    activated = (jax.nn.silu(gate_pre) * up_pre).astype(jnp.bfloat16)
    answer = jnp.dot(activated, w_down, preferred_element_type=jnp.float32)
    return answer * gate[:, None]


MESH = pl.DeviceIdType.MESH


def spans_of(token_count, blocks):
    longest = token_count * blocks // 3
    reach = min(blocks - 1, max(1, (longest - 2) // token_count + 1))
    spans = []
    while sum(spans) < reach:
        spans.append(2 ** len(spans))
    return spans


def attn_kernel(
    blocks,
    spans,
    q_ref,
    k_ref,
    v_ref,
    seg_col,
    seg_row,
    map_ref,
    gain_ref,
    out_ref,
    key_feat,
    query_feat,
    window,
    carried,
    within,
    outbox,
    inbox,
    seg_out,
    seg_in,
    send_sem,
    recv_sem,
    seg_send,
    seg_recv,
):
    tokens = q_ref.shape[0]
    heads, dim, _ = map_ref.shape
    place = lax.axis_index("seq")
    f32, bf16 = jnp.float32, jnp.bfloat16

    barrier = pltpu.get_barrier_semaphore()
    for span in spans:
        for shift in (span, blocks - span):
            other = (place + shift) % blocks
            pl.semaphore_signal(barrier, inc=1, device_id={"seq": other}, device_id_type=MESH)
    pl.semaphore_wait(barrier, 2 * len(spans))

    def packet(i, h):
        return pltpu.make_async_remote_copy(
            src_ref=outbox.at[i, h],
            dst_ref=inbox.at[i, h],
            send_sem=send_sem.at[i, h],
            recv_sem=recv_sem.at[i, h],
            device_id={"seq": place + spans[i]},
            device_id_type=MESH,
        )

    def note(i):
        return pltpu.make_async_remote_copy(
            src_ref=seg_out,
            dst_ref=seg_in.at[i],
            send_sem=seg_send.at[i],
            recv_sem=seg_recv.at[i],
            device_id={"seq": place + spans[i]},
            device_id_type=MESH,
        )

    last = seg_col[tokens - 1 : tokens, :]
    seg_out[...] = jnp.broadcast_to(last.astype(f32), seg_out.shape)
    for i, span in enumerate(spans):

        @pl.when(place + span < blocks)
        def _tell(i=i):
            note(i).start()

        @pl.when(place < span)
        def _none(i=i):
            seg_in[i] = jnp.full(seg_in.shape[1:], -1.0, f32)
            inbox[i] = jnp.zeros(inbox.shape[1:], bf16)

    def features(x, h):
        projected = jnp.dot(x, map_ref[h], preferred_element_type=f32)
        return jnp.where(projected > 0, projected + 1.0, jnp.exp(jnp.minimum(projected, 0.0))).astype(
            bf16
        )

    def lanes(h):
        return pl.ds(pl.multiple_of(h * dim, dim), dim)

    def send(i, h):
        outbox[i, h] = window[h].astype(bf16)

        @pl.when(place + spans[i] < blocks)
        def _go():
            packet(i, h).start()

    tail = seg_col[...] == last

    def key_step(h, carry):
        feat = features(k_ref[:, lanes(h)], h)
        key_feat[h] = feat
        tail_values = jnp.where(tail, v_ref[:, lanes(h)].astype(f32), 0.0).astype(bf16)
        window[h] = lax.dot_general(
            feat, tail_values, (((0,), (0,)), ((), ())), preferred_element_type=f32
        )
        send(0, h)
        return carry

    lax.fori_loop(0, heads, key_step, 0)
    for i, span in enumerate(spans):

        @pl.when(place >= span)
        def _told(i=i):
            note(i).wait_recv()

    last_f = last.astype(f32)
    before = seg_in[0, 0:1, 0:1]
    reached = seg_col[...].astype(f32) == before
    row = lax.broadcasted_iota(jnp.int32, (tokens, tokens), 0)
    col = lax.broadcasted_iota(jnp.int32, (tokens, tokens), 1)
    allowed = (col <= row) & (seg_col[...] == seg_row[...])

    def take(i, h):
        @pl.when(place >= spans[i])
        def _arrived():
            packet(i, h).wait_recv()

        shifted = inbox[i, h].astype(f32)
        seg = seg_in[i, 0:1, 0:1]
        if i == 0:
            carried[h] = shifted
        else:
            carried[h] = carried[h] + jnp.where(seg == before, shifted, 0.0)
        if i + 1 < len(spans):
            window[h] = window[h] + jnp.where(seg == last_f, shifted, 0.0)
            send(i + 1, h)

    def finish(h):
        far = jnp.dot(query_feat[h], carried[h].astype(bf16), preferred_element_type=f32)
        mixed = within[:, lanes(h)] + jnp.where(reached, far, 0.0)
        scale = lax.rsqrt(jnp.mean(mixed * mixed, axis=1, keepdims=True) + 1e-06)
        out_ref[:, lanes(h)] = (mixed * scale * gain_ref[:, lanes(h)]).astype(bf16)

    def query_step(h, carry):
        feat = features(q_ref[:, lanes(h)], h)
        query_feat[h] = feat
        scores = lax.dot_general(
            feat, key_feat[h], (((1,), (1,)), ((), ())), preferred_element_type=f32
        )
        weights = jnp.where(allowed, scores, 0.0).astype(bf16)
        within[:, lanes(h)] = jnp.dot(weights, v_ref[:, lanes(h)], preferred_element_type=f32)
        take(0, h)
        return carry

    lax.fori_loop(0, heads, query_step, 0)
    for i in range(1, len(spans)):

        def later_step(h, carry, i=i):
            take(i, h)
            if i == len(spans) - 1:
                finish(h)
            return carry

        lax.fori_loop(0, heads, later_step, 0)
    if len(spans) == 1:

        def last_step(h, carry):
            finish(h)
            return carry

        lax.fori_loop(0, heads, last_step, 0)

    for i, span in enumerate(spans):

        @pl.when(place + span < blocks)
        def _sent(i=i):
            note(i).wait_send()

            def done_step(h, carry):
                packet(i, h).wait_send()
                return carry

            lax.fori_loop(0, heads, done_step, 0)


def attention(query_proj, key_proj, value_proj, segment_ids, feature_map, head_gain):
    tokens = query_proj.shape[0]
    heads, dim, feat = feature_map.shape
    blocks = lax.axis_size("seq")
    spans = spans_of(tokens, blocks)
    count = len(spans)
    dma = pltpu.SemaphoreType.DMA
    f32, bf16 = jnp.float32, jnp.bfloat16
    return pl.pallas_call(
        functools.partial(attn_kernel, blocks, spans),
        out_shape=jax.ShapeDtypeStruct((tokens, heads * dim), bf16),
        in_specs=[pl.BlockSpec(memory_space=pltpu.VMEM)] * 7,
        out_specs=pl.BlockSpec(memory_space=pltpu.VMEM),
        scratch_shapes=[
            pltpu.VMEM((heads, tokens, feat), bf16),
            pltpu.VMEM((heads, tokens, feat), bf16),
            pltpu.VMEM((heads, feat, dim), f32),
            pltpu.VMEM((heads, feat, dim), f32),
            pltpu.VMEM((tokens, heads * dim), f32),
            pltpu.VMEM((count, heads, feat, dim), bf16),
            pltpu.VMEM((count, heads, feat, dim), bf16),
            pltpu.VMEM((8, 128), f32),
            pltpu.VMEM((count, 8, 128), f32),
            dma((count, heads)),
            dma((count, heads)),
            dma((count,)),
            dma((count,)),
        ],
        compiler_params=pltpu.CompilerParams(
            collective_id=1, has_side_effects=True, vmem_limit_bytes=32 * 1024 * 1024
        ),
    )(
        query_proj,
        key_proj,
        value_proj,
        segment_ids.reshape(tokens, 1),
        segment_ids.reshape(1, tokens),
        feature_map,
        head_gain.reshape(1, heads * dim),
    )


TILE = 256
VMEM_MOST = 63 * 1024 * 1024


def ring_place(index, count, folded):
    if not folded:
        return index
    far, side = index // 2, index % 2
    return far + side * (count - 1 - 2 * far)


def ring_index(place, count, folded):
    if not folded:
        return place
    side = place // (count // 2)
    far = place + side * (count - 1 - 2 * place)
    return 2 * far + side


def moe_kernel(
    count,
    folded,
    experts,
    x_ref,
    wg_hbm,
    wu_hbm,
    wd_hbm,
    out_ref,
    rows_buf,
    part,
    pair,
    inbox,
    wg,
    wu,
    wd,
    act,
    load_sem,
    ag_send,
    ag_recv,
    sib_send,
    sib_recv,
    rs_send,
    rs_recv,
    pair_send,
    pair_recv,
):
    rows, padded = x_ref.shape
    width = out_ref.shape[1]
    half = rows // 2
    far = count // 2
    core = lax.axis_index("head")
    seq = lax.axis_index("seq")
    place = ring_place(seq, count, folded)
    ahead = {"seq": ring_index((place + 1) % count, count, folded)}
    behind = {"seq": ring_index((place + count - 1) % count, count, folded)}
    sibling = {"head": 1 - core}
    toward = (ahead, behind)

    loads = [
        pltpu.make_async_copy(src.at[0], dst, load_sem.at[i])
        for i, (src, dst) in enumerate(((wg_hbm, wg), (wu_hbm, wu), (wd_hbm, wd)))
    ]
    for load in loads:
        load.start()

    barrier = pltpu.get_barrier_semaphore()
    for other in (ahead, behind, sibling):
        pl.semaphore_signal(barrier, inc=1, device_id=other, device_id_type=MESH)
    pl.semaphore_wait(barrier, 3)

    def spot(slot):
        if slot == 0:
            return 0
        if slot == far:
            return count - 1
        return 2 * slot - 1 if slot < far else 2 * (count - slot)

    def start_row(slot, which, part_of=0):
        return pl.multiple_of((spot(slot) * 2 + which) * rows + part_of * half, half)

    def block(ref, slot, which):
        return ref.at[pl.ds(start_row(slot, which), rows)]

    def chunk(ref, slot, which, h):
        return ref.at[pl.ds(start_row(slot, which, h), half)]

    def slot_of(way, hop):
        return hop if way == 0 else (count - hop) % count

    own_copy = pltpu.make_async_copy(x_ref, block(rows_buf, 0, core), load_sem.at[3])
    own_copy.start()

    gathers = {}
    for way in range(2):
        for hop in range(far):
            for h in range(2):
                if hop == far - 1 and h != way:
                    continue
                if hop == 0:
                    src = x_ref.at[pl.ds(h * half, half)]
                else:
                    src = chunk(rows_buf, slot_of(way, hop), core, h)
                gathers[way, hop, h] = pltpu.make_async_remote_copy(
                    src_ref=src,
                    dst_ref=chunk(rows_buf, slot_of(way, hop + 1), core, h),
                    send_sem=ag_send.at[way, hop, h],
                    recv_sem=ag_recv.at[way, hop, h],
                    device_id=toward[way],
                    device_id_type=MESH,
                )

    shares = {}
    answers = {}
    for slot in range(count):
        src = x_ref if slot == 0 else block(rows_buf, slot, core)
        shares[slot] = pltpu.make_async_remote_copy(
            src_ref=src,
            dst_ref=block(rows_buf, slot, core),
            send_sem=sib_send.at[slot],
            recv_sem=sib_recv.at[slot],
            device_id=sibling,
            device_id_type=MESH,
        )
        answers[slot] = pltpu.make_async_remote_copy(
            src_ref=block(part, slot, 1 - core),
            dst_ref=pair.at[slot],
            send_sem=pair_send.at[slot],
            recv_sem=pair_recv.at[slot],
            device_id=sibling,
            device_id_type=MESH,
        )

    def compute(first_slot, blocks):
        low = spot(first_slot) * 2 * rows
        tall = blocks * 2 * rows
        expert = lax.axis_index("seq") * 2 + core
        taken = pl.ds(low, tall)
        extra = rows_buf[taken, width:].astype(jnp.float32)
        lane = lax.broadcasted_iota(jnp.int32, extra.shape, 1)
        mine = (lane == expert) | (lane == expert + experts)
        gate = jnp.sum(jnp.where(mine, extra, 0.0), axis=1, keepdims=True)

        def up_step(t, carry):
            cols = pl.ds(pl.multiple_of(t * TILE, TILE), TILE)
            x = rows_buf[taken, :width]
            gate_pre = jnp.dot(x, wg[:, cols], preferred_element_type=jnp.float32)
            up_pre = jnp.dot(x, wu[:, cols], preferred_element_type=jnp.float32)
            act[:tall, cols] = (gate_pre * jax.nn.sigmoid(gate_pre) * up_pre).astype(jnp.bfloat16)
            return carry

        lax.fori_loop(0, wg.shape[1] // TILE, up_step, 0)

        def down_step(t, carry):
            cols = pl.ds(pl.multiple_of(t * TILE, TILE), TILE)
            answer = jnp.dot(act[:tall, :], wd[:, cols], preferred_element_type=jnp.float32)
            part[taken, cols] = (answer * gate).astype(jnp.bfloat16)
            return carry

        lax.fori_loop(0, width // TILE, down_step, 0)

    sums = {}
    for way in range(2):
        for hop in range(far, 0, -1):
            for h in range(2):
                if hop == far and h != way:
                    continue
                sums[way, hop, h] = pltpu.make_async_remote_copy(
                    src_ref=chunk(part, slot_of(way, hop), core, h),
                    dst_ref=inbox.at[way, hop - 1, h],
                    send_sem=rs_send.at[way, hop - 1, h],
                    recv_sem=rs_recv.at[way, hop - 1, h],
                    device_id=toward[1 - way],
                    device_id_type=MESH,
                )

    def add_and_send(way, hop, h):
        slot = slot_of(way, hop)
        here = pl.ds(start_row(slot, core, h), half)
        total = part[here, :].astype(jnp.float32) + pair[slot, h * half : (h + 1) * half, :].astype(
            jnp.float32
        )
        if (way, hop + 1, h) in sums:
            sums[way, hop + 1, h].wait_recv()
            total = total + inbox[way, hop, h].astype(jnp.float32)
        part[here, :] = total.astype(jnp.bfloat16)
        sums[way, hop, h].start()

    for h in range(2):
        for way in range(2):
            at = h if way == 0 else 1 - h
            if (way, 0, at) in gathers:
                gathers[way, 0, at].start()
    shares[0].start()
    for load in loads:
        load.wait()
    own_copy.wait()
    shares[0].wait_recv()
    compute(0, 1)
    answers[0].start()
    for hop in range(1, far + 1):
        for h in range(2):
            for way in range(2):
                at = h if way == 0 else 1 - h
                if (way, hop - 1, at) in gathers:
                    gathers[way, hop - 1, at].wait_recv()
                if (way, hop, at) in gathers:
                    gathers[way, hop, at].start()
        slots = (hop, count - hop) if hop < far else (far,)
        for slot in slots:
            shares[slot].start()
        for slot in slots:
            shares[slot].wait_recv()
        compute(hop, len(slots))
        for slot in slots:
            answers[slot].start()
        if hop == far - 1:
            for way in range(2):
                answers[slot_of(way, hop)].wait_recv()
            for way in range(2):
                add_and_send(way, hop, 1 - way)

    answers[far].wait_recv()
    for way in range(2):
        add_and_send(way, far, way)
    for way in range(2):
        add_and_send(way, far - 1, way)
    for hop in range(far - 2, 0, -1):
        for way in range(2):
            answers[slot_of(way, hop)].wait_recv()
        for turn in range(2):
            for way in range(2):
                add_and_send(way, hop, 1 - way if turn == 0 else way)
    answers[0].wait_recv()
    for h in range(2):
        here = pl.ds(start_row(0, core, h), half)
        total = part[here, :].astype(jnp.float32) + pair[0, h * half : (h + 1) * half, :].astype(
            jnp.float32
        )
        for way in range(2):
            if (way, 1, h) in sums:
                sums[way, 1, h].wait_recv()
                total = total + inbox[way, 0, h].astype(jnp.float32)
        out_ref[h * half : (h + 1) * half, :] = total.astype(out_ref.dtype)
    for group in (gathers, shares, answers, sums):
        for copy in group.values():
            copy.wait_send()


def moe_scratch(count, rows, padded, width, hidden):
    half = rows // 2
    far = count // 2
    tall = count * 2 * rows
    bf16 = jnp.bfloat16
    return [
        ((tall, padded), bf16),
        ((tall, width), bf16),
        ((count, rows, width), bf16),
        ((2, far, 2, half, width), bf16),
        ((width, hidden), bf16),
        ((width, hidden), bf16),
        ((hidden, width), bf16),
        ((4 * rows, hidden), bf16),
    ]


def moe(rows_in, width, experts, w_gate, w_up, w_down, folded):
    count = lax.axis_size("seq")
    rows, padded = rows_in.shape
    far = count // 2
    dma = pltpu.SemaphoreType.DMA
    scratch = moe_scratch(count, rows, padded, width, w_gate.shape[2])
    tall = count * 2 * rows
    return pl.pallas_call(
        functools.partial(moe_kernel, count, folded, experts),
        out_shape=jax.ShapeDtypeStruct((rows, width), jnp.bfloat16),
        in_specs=[pl.BlockSpec(memory_space=pltpu.VMEM)]
        + [pl.BlockSpec(memory_space=pl.ANY)] * 3,
        out_specs=pl.BlockSpec(memory_space=pltpu.VMEM),
        scratch_shapes=[pltpu.VMEM(shape, dtype) for shape, dtype in scratch]
        + [
            dma((4,)),
            dma((2, far, 2)),
            dma((2, far, 2)),
            dma((count,)),
            dma((count,)),
            dma((2, far, 2)),
            dma((2, far, 2)),
            dma((count,)),
            dma((count,)),
        ],
        compiler_params=pltpu.CompilerParams(
            collective_id=0, has_side_effects=True, vmem_limit_bytes=VMEM_MOST
        ),
        cost_estimate=pl.CostEstimate(
            flops=6 * tall * width * w_gate.shape[2],
            bytes_accessed=6 * width * w_gate.shape[2],
            transcendentals=tall * w_gate.shape[2],
        ),
    )(rows_in, w_gate, w_up, w_down)


def moe_fits(count, heads, rows, padded, width, w_gate):
    if heads != 2 or count < 4 or count % 2 or w_gate.shape[0] != 1:
        return False
    if rows % 32 or width % TILE or w_gate.shape[2] % TILE:
        return False
    need = 0
    for shape, _ in moe_scratch(count, rows, padded, width, w_gate.shape[2]):
        size = 2
        for extent in shape:
            size *= extent
        need += size
    return need < VMEM_MOST * 7 // 8


def shards(
    folded,
    query_proj,
    key_proj,
    value_proj,
    segment_ids,
    feature_map,
    head_gain,
    residual,
    out_weight,
    norm_gain,
    router,
    w_gate,
    w_up,
    w_down,
    expert_ids,
):
    attn_heads = attention(query_proj, key_proj, value_proj, segment_ids, feature_map, head_gain)
    row_count = residual.shape[0]
    head_place = lax.axis_index("head")
    head_devs = lax.axis_size("head")
    sums = jnp.dot(attn_heads, out_weight, preferred_element_type=jnp.float32)
    projected = lax.dynamic_slice_in_dim(sums, head_place * row_count, row_count)
    for step in range(1, head_devs):
        target = (head_place + step) % head_devs
        projected = projected + lax.ppermute(
            lax.dynamic_slice_in_dim(sums, target * row_count, row_count),
            "head",
            [(i, (i + step) % head_devs) for i in range(head_devs)],
        )
    hidden = (residual.astype(jnp.float32) + projected).astype(jnp.bfloat16)
    hidden_f = hidden.astype(jnp.float32)
    normed = (
        hidden_f
        * lax.rsqrt(jnp.mean(hidden_f * hidden_f, axis=1, keepdims=True) + 1e-05)
        * norm_gain
    ).astype(jnp.bfloat16)
    logits = jnp.dot(normed, router, preferred_element_type=jnp.float32)
    expert_count = router.shape[1]
    expert_iota = lax.iota(jnp.int32, expert_count)
    picked = expert_ids[:, :, None] == expert_iota[None, None, :]
    chosen = jnp.sum(jnp.where(picked, logits[:, None, :], 0.0), axis=2)
    gates = jax.nn.sigmoid(chosen)
    gate_weights = gates / jnp.sum(gates, axis=1, keepdims=True)
    dense_gates = jnp.sum(jnp.where(picked, gate_weights[:, :, None], 0.0), axis=1)
    model_width = normed.shape[1]
    coarse = lax.reduce_precision(dense_gates, 8, 7)
    lanes = -(-2 * expert_count // 128) * 128
    extra = jnp.concatenate([coarse, dense_gates - coarse], axis=1).astype(jnp.bfloat16)
    extra = jnp.pad(extra, ((0, 0), (0, lanes - 2 * expert_count)))
    if moe_fits(lax.axis_size("seq"), head_devs, row_count, model_width + lanes, model_width, w_gate):
        rows_in = jnp.concatenate([normed, extra], axis=1)
        expert_sum = moe(rows_in, model_width, expert_count, w_gate, w_up, w_down, folded)
        return (hidden, expert_sum)
    spread = ("seq", "head")
    all_rows = lax.all_gather(normed, spread, axis=0, tiled=True)
    all_gates = lax.all_gather(dense_gates, spread, axis=0, tiled=True)
    exp_dev = w_gate.shape[0]
    first = (lax.axis_index("seq") * lax.axis_size("head") + lax.axis_index("head")) * exp_dev
    partial = 0.0
    for own in range(exp_dev):
        gate = jnp.sum(jnp.where(expert_iota[None, :] == first + own, all_gates, 0.0), axis=1)
        partial = partial + run_expert(all_rows, gate, w_gate[own], w_up[own], w_down[own])
    expert_sum = lax.psum_scatter(
        partial.astype(jnp.bfloat16), spread, scatter_dimension=0, tiled=True
    )
    return (hidden, expert_sum)


def folded_seq(mesh):
    chips = [getattr(d, "coords", None) for d in mesh.devices[0, :3, 0]]
    if None in chips or len(chips) < 3:
        return True
    moved = [sum(abs(i - j) for i, j in zip(a, b)) for a, b in zip(chips, chips[1:])]
    return moved[0] == 1 and moved[1] == 2


def solution(mesh):
    placed = (
        P(("groups", "seq"), "head"),
        P(("groups", "seq"), "head"),
        P(("groups", "seq"), "head"),
        P(("groups", "seq")),
        P("head", None, None),
        P("head"),
        P(("groups", "seq", "head"), None),
        P("head", None),
        P(),
        P(),
        P(("seq", "head"), None, None),
        P(("seq", "head"), None, None),
        P(("seq", "head"), None, None),
        P(("groups", "seq", "head"), None),
    )
    return jax.shard_map(
        functools.partial(shards, folded_seq(mesh)),
        mesh=mesh,
        in_specs=placed,
        out_specs=(P(("groups", "seq", "head"), None), P(("groups", "seq", "head"), None)),
        check_vma=False,
    )
```

```python
import functools

import jax
import jax.numpy as jnp
from jax import lax
from jax.experimental import pallas as pl
from jax.experimental.pallas import tpu as pltpu
from jax.sharding import PartitionSpec as P


def run_expert(rows, gate, w_gate, w_up, w_down):
    gate_pre = jnp.dot(rows, w_gate, preferred_element_type=jnp.float32)
    up_pre = jnp.dot(rows, w_up, preferred_element_type=jnp.float32)
    activated = (jax.nn.silu(gate_pre) * up_pre).astype(jnp.bfloat16)
    answer = jnp.dot(activated, w_down, preferred_element_type=jnp.float32)
    return answer * gate[:, None]


MESH = pl.DeviceIdType.MESH


def spans_of(token_count, blocks):
    longest = token_count * blocks // 3
    reach = min(blocks - 1, max(1, (longest - 2) // token_count + 1))
    spans = []
    while sum(spans) < reach:
        spans.append(2 ** len(spans))
    return spans


def attn_kernel(
    blocks,
    spans,
    q_hbm,
    k_hbm,
    v_hbm,
    seg_col,
    seg_row,
    map_hbm,
    gain_ref,
    out_ref,
    q_ref,
    k_ref,
    v_ref,
    map_ref,
    load_sem,
    key_feat,
    query_feat,
    window,
    carried,
    within,
    outbox,
    inbox,
    seg_out,
    seg_in,
    send_sem,
    recv_sem,
    seg_send,
    seg_recv,
):
    tokens = q_ref.shape[0]
    heads, dim, _ = map_ref.shape
    place = lax.axis_index("seq")
    f32, bf16 = jnp.float32, jnp.bfloat16

    sources = ((k_hbm, k_ref), (map_hbm, map_ref), (v_hbm, v_ref), (q_hbm, q_ref))
    loads = [
        pltpu.make_async_copy(src, dst, load_sem.at[i]) for i, (src, dst) in enumerate(sources)
    ]
    for load in loads:
        load.start()

    barrier = pltpu.get_barrier_semaphore()
    for span in spans:
        for shift in (span, blocks - span):
            other = (place + shift) % blocks
            pl.semaphore_signal(barrier, inc=1, device_id={"seq": other}, device_id_type=MESH)
    pl.semaphore_wait(barrier, 2 * len(spans))

    def packet(i, h):
        return pltpu.make_async_remote_copy(
            src_ref=outbox.at[i, h],
            dst_ref=inbox.at[i, h],
            send_sem=send_sem.at[i, h],
            recv_sem=recv_sem.at[i, h],
            device_id={"seq": place + spans[i]},
            device_id_type=MESH,
        )

    def note(i):
        return pltpu.make_async_remote_copy(
            src_ref=seg_out,
            dst_ref=seg_in.at[i],
            send_sem=seg_send.at[i],
            recv_sem=seg_recv.at[i],
            device_id={"seq": place + spans[i]},
            device_id_type=MESH,
        )

    last = seg_col[tokens - 1 : tokens, :]
    seg_out[...] = jnp.broadcast_to(last.astype(f32), seg_out.shape)
    for i, span in enumerate(spans):

        @pl.when(place + span < blocks)
        def _tell(i=i):
            note(i).start()

        @pl.when(place < span)
        def _none(i=i):
            seg_in[i] = jnp.full(seg_in.shape[1:], -1.0, f32)
            inbox[i] = jnp.zeros(inbox.shape[1:], bf16)

    def features(x, h):
        projected = jnp.dot(x, map_ref[h], preferred_element_type=f32)
        return jnp.where(projected > 0, projected + 1.0, jnp.exp(jnp.minimum(projected, 0.0))).astype(
            bf16
        )

    def lanes(h):
        return pl.ds(pl.multiple_of(h * dim, dim), dim)

    def send(i, h):
        outbox[i, h] = window[h].astype(bf16)

        @pl.when(place + spans[i] < blocks)
        def _go():
            packet(i, h).start()

    tail = seg_col[...] == last

    def key_step(h, carry):
        feat = features(k_ref[:, lanes(h)], h)
        key_feat[h] = feat
        tail_values = jnp.where(tail, v_ref[:, lanes(h)].astype(f32), 0.0).astype(bf16)
        window[h] = lax.dot_general(
            feat, tail_values, (((0,), (0,)), ((), ())), preferred_element_type=f32
        )
        send(0, h)
        return carry

    for load in loads[:3]:
        load.wait()
    lax.fori_loop(0, heads, key_step, 0)
    loads[3].wait()
    for i, span in enumerate(spans):

        @pl.when(place >= span)
        def _told(i=i):
            note(i).wait_recv()

    last_f = last.astype(f32)
    before = seg_in[0, 0:1, 0:1]
    reached = seg_col[...].astype(f32) == before
    row = lax.broadcasted_iota(jnp.int32, (tokens, tokens), 0)
    col = lax.broadcasted_iota(jnp.int32, (tokens, tokens), 1)
    allowed = (col <= row) & (seg_col[...] == seg_row[...])

    def take(i, h):
        @pl.when(place >= spans[i])
        def _arrived():
            packet(i, h).wait_recv()

        shifted = inbox[i, h].astype(f32)
        seg = seg_in[i, 0:1, 0:1]
        if i == 0:
            carried[h] = shifted
        else:
            carried[h] = carried[h] + jnp.where(seg == before, shifted, 0.0)
        if i + 1 < len(spans):
            window[h] = window[h] + jnp.where(seg == last_f, shifted, 0.0)
            send(i + 1, h)

    def finish(h):
        far = jnp.dot(query_feat[h], carried[h].astype(bf16), preferred_element_type=f32)
        mixed = within[:, lanes(h)] + jnp.where(reached, far, 0.0)
        scale = lax.rsqrt(jnp.mean(mixed * mixed, axis=1, keepdims=True) + 1e-06)
        out_ref[:, lanes(h)] = (mixed * scale * gain_ref[:, lanes(h)]).astype(bf16)

    def query_step(h, carry):
        feat = features(q_ref[:, lanes(h)], h)
        query_feat[h] = feat
        scores = lax.dot_general(
            feat, key_feat[h], (((1,), (1,)), ((), ())), preferred_element_type=f32
        )
        weights = jnp.where(allowed, scores, 0.0).astype(bf16)
        within[:, lanes(h)] = jnp.dot(weights, v_ref[:, lanes(h)], preferred_element_type=f32)
        take(0, h)
        return carry

    lax.fori_loop(0, heads, query_step, 0)
    for i in range(1, len(spans)):

        def later_step(h, carry, i=i):
            take(i, h)
            if i == len(spans) - 1:
                finish(h)
            return carry

        lax.fori_loop(0, heads, later_step, 0)
    if len(spans) == 1:

        def last_step(h, carry):
            finish(h)
            return carry

        lax.fori_loop(0, heads, last_step, 0)

    for i, span in enumerate(spans):

        @pl.when(place + span < blocks)
        def _sent(i=i):
            note(i).wait_send()

            def done_step(h, carry):
                packet(i, h).wait_send()
                return carry

            lax.fori_loop(0, heads, done_step, 0)


def attention(query_proj, key_proj, value_proj, segment_ids, feature_map, head_gain):
    tokens = query_proj.shape[0]
    heads, dim, feat = feature_map.shape
    blocks = lax.axis_size("seq")
    spans = spans_of(tokens, blocks)
    count = len(spans)
    dma = pltpu.SemaphoreType.DMA
    f32, bf16 = jnp.float32, jnp.bfloat16
    in_any = pl.BlockSpec(memory_space=pl.ANY)
    in_vmem = pl.BlockSpec(memory_space=pltpu.VMEM)
    return pl.pallas_call(
        functools.partial(attn_kernel, blocks, spans),
        out_shape=jax.ShapeDtypeStruct((tokens, heads * dim), bf16),
        in_specs=[in_any, in_any, in_any, in_vmem, in_vmem, in_any, in_vmem],
        out_specs=pl.BlockSpec(memory_space=pltpu.VMEM),
        scratch_shapes=[
            pltpu.VMEM(query_proj.shape, bf16),
            pltpu.VMEM(key_proj.shape, bf16),
            pltpu.VMEM(value_proj.shape, bf16),
            pltpu.VMEM(feature_map.shape, bf16),
            dma((4,)),
            pltpu.VMEM((heads, tokens, feat), bf16),
            pltpu.VMEM((heads, tokens, feat), bf16),
            pltpu.VMEM((heads, feat, dim), f32),
            pltpu.VMEM((heads, feat, dim), f32),
            pltpu.VMEM((tokens, heads * dim), f32),
            pltpu.VMEM((count, heads, feat, dim), bf16),
            pltpu.VMEM((count, heads, feat, dim), bf16),
            pltpu.VMEM((8, 128), f32),
            pltpu.VMEM((count, 8, 128), f32),
            dma((count, heads)),
            dma((count, heads)),
            dma((count,)),
            dma((count,)),
        ],
        compiler_params=pltpu.CompilerParams(
            collective_id=1, has_side_effects=True, vmem_limit_bytes=32 * 1024 * 1024
        ),
    )(
        query_proj,
        key_proj,
        value_proj,
        segment_ids.reshape(tokens, 1),
        segment_ids.reshape(1, tokens),
        feature_map,
        head_gain.reshape(1, heads * dim),
    )


TILE = 256
VMEM_MOST = 63 * 1024 * 1024


def ring_place(index, count, folded):
    if not folded:
        return index
    far, side = index // 2, index % 2
    return far + side * (count - 1 - 2 * far)


def ring_index(place, count, folded):
    if not folded:
        return place
    side = place // (count // 2)
    far = place + side * (count - 1 - 2 * place)
    return 2 * far + side


def moe_kernel(
    count,
    folded,
    experts,
    taken_most,
    x_ref,
    wg_hbm,
    wu_hbm,
    wd_hbm,
    out_ref,
    rows_buf,
    part,
    pair,
    inbox,
    wg,
    wu,
    wd,
    act,
    packed,
    load_sem,
    ag_send,
    ag_recv,
    sib_send,
    sib_recv,
    rs_send,
    rs_recv,
    pair_send,
    pair_recv,
):
    rows, padded = x_ref.shape
    width = out_ref.shape[1]
    half = rows // 2
    far = count // 2
    core = lax.axis_index("head")
    seq = lax.axis_index("seq")
    place = ring_place(seq, count, folded)
    ahead = {"seq": ring_index((place + 1) % count, count, folded)}
    behind = {"seq": ring_index((place + count - 1) % count, count, folded)}
    sibling = {"head": 1 - core}
    toward = (ahead, behind)

    loads = [
        pltpu.make_async_copy(src.at[0], dst, load_sem.at[i])
        for i, (src, dst) in enumerate(((wg_hbm, wg), (wu_hbm, wu), (wd_hbm, wd)))
    ]
    for load in loads:
        load.start()

    barrier = pltpu.get_barrier_semaphore()
    for other in (ahead, behind, sibling):
        pl.semaphore_signal(barrier, inc=1, device_id=other, device_id_type=MESH)
    pl.semaphore_wait(barrier, 3)

    def spot(slot):
        if slot == 0:
            return 0
        if slot == far:
            return count - 1
        return 2 * slot - 1 if slot < far else 2 * (count - slot)

    def start_row(slot, which, part_of=0):
        return pl.multiple_of((spot(slot) * 2 + which) * rows + part_of * half, half)

    def block(ref, slot, which):
        return ref.at[pl.ds(start_row(slot, which), rows)]

    def chunk(ref, slot, which, h):
        return ref.at[pl.ds(start_row(slot, which, h), half)]

    def slot_of(way, hop):
        return hop if way == 0 else (count - hop) % count

    own_copy = pltpu.make_async_copy(x_ref, block(rows_buf, 0, core), load_sem.at[3])
    own_copy.start()

    gathers = {}
    for way in range(2):
        for hop in range(far):
            for h in range(2):
                if hop == far - 1 and h != way:
                    continue
                if hop == 0:
                    src = x_ref.at[pl.ds(h * half, half)]
                else:
                    src = chunk(rows_buf, slot_of(way, hop), core, h)
                gathers[way, hop, h] = pltpu.make_async_remote_copy(
                    src_ref=src,
                    dst_ref=chunk(rows_buf, slot_of(way, hop + 1), core, h),
                    send_sem=ag_send.at[way, hop, h],
                    recv_sem=ag_recv.at[way, hop, h],
                    device_id=toward[way],
                    device_id_type=MESH,
                )

    shares = {}
    answers = {}
    for slot in range(count):
        src = x_ref if slot == 0 else block(rows_buf, slot, core)
        shares[slot] = pltpu.make_async_remote_copy(
            src_ref=src,
            dst_ref=block(rows_buf, slot, core),
            send_sem=sib_send.at[slot],
            recv_sem=sib_recv.at[slot],
            device_id=sibling,
            device_id_type=MESH,
        )
        answers[slot] = pltpu.make_async_remote_copy(
            src_ref=block(part, slot, 1 - core),
            dst_ref=pair.at[slot],
            send_sem=pair_send.at[slot],
            recv_sem=pair_recv.at[slot],
            device_id=sibling,
            device_id_type=MESH,
        )

    def compute(first_slot, blocks):
        pair_rows = 2 * rows
        expert = lax.axis_index("seq") * 2 + core
        f32, bf16 = jnp.float32, jnp.bfloat16
        row = lax.broadcasted_iota(jnp.int32, (pair_rows, pair_rows), 0)
        col = lax.broadcasted_iota(jnp.int32, (pair_rows, pair_rows), 1)
        earlier_row = jnp.where(row < col, 1.0, 0.0).astype(bf16)
        earlier_col = jnp.where(col < row, 1.0, 0.0).astype(bf16)
        slot_down = lax.broadcasted_iota(jnp.int32, (taken_most, pair_rows), 0).astype(f32)
        slot_across = lax.broadcasted_iota(jnp.int32, (pair_rows, taken_most), 1).astype(f32)
        ones = jnp.ones((8, padded - width), bf16)
        gates, backs, places = [], [], []
        for j in range(blocks):
            taken = pl.ds(spot(first_slot) * pair_rows + j * pair_rows, pair_rows)
            extra = rows_buf[taken, width:].astype(f32)
            lane = lax.broadcasted_iota(jnp.int32, extra.shape, 1)
            mine = (lane == expert) | (lane == expert + experts)
            gate = jnp.sum(jnp.where(mine, extra, 0.0), axis=1, keepdims=True)
            named = jnp.where((lane == expert) & (gate > 0), 1.0, 0.0)
            named_col = jnp.sum(named, axis=1, keepdims=True)
            named = named.astype(bf16)
            named_row = lax.dot_general(
                ones, named, (((1,), (1,)), ((), ())), preferred_element_type=f32
            )
            ahead_row = jnp.dot(named_row.astype(bf16), earlier_row, preferred_element_type=f32)
            ahead_col = jnp.sum(
                jnp.dot(earlier_col, named, preferred_element_type=f32), axis=1, keepdims=True
            )
            pick = jnp.where((slot_down == ahead_row[0:1]) & (named_row[0:1] > 0), 1.0, 0.0)
            back = jnp.where((slot_across == ahead_col) & (named_col > 0), 1.0, 0.0)
            pick = pick.astype(bf16)
            gates.append(gate)
            backs.append(back.astype(bf16))
            places.append(taken)

            def pack_step(t, carry, j=j, pick=pick, taken=taken):
                cols = pl.ds(pl.multiple_of(t * TILE, TILE), TILE)
                packed[j * taken_most : (j + 1) * taken_most, cols] = jnp.dot(
                    pick, rows_buf[taken, cols], preferred_element_type=f32
                ).astype(bf16)
                return carry

            lax.fori_loop(0, width // TILE, pack_step, 0)
        tall = blocks * taken_most

        def up_step(t, carry):
            cols = pl.ds(pl.multiple_of(t * TILE, TILE), TILE)
            x = packed[:tall, :]
            gate_pre = jnp.dot(x, wg[:, cols], preferred_element_type=f32)
            up_pre = jnp.dot(x, wu[:, cols], preferred_element_type=f32)
            act[:tall, cols] = (gate_pre * jax.nn.sigmoid(gate_pre) * up_pre).astype(bf16)
            return carry

        lax.fori_loop(0, wg.shape[1] // TILE, up_step, 0)

        def down_step(t, carry):
            cols = pl.ds(pl.multiple_of(t * TILE, TILE), TILE)
            answer = jnp.dot(act[:tall, :], wd[:, cols], preferred_element_type=f32).astype(bf16)
            for j in range(blocks):
                own = answer[j * taken_most : (j + 1) * taken_most]
                spread = jnp.dot(backs[j], own, preferred_element_type=f32)
                part[places[j], cols] = (spread * gates[j]).astype(bf16)
            return carry

        lax.fori_loop(0, width // TILE, down_step, 0)

    sums = {}
    for way in range(2):
        for hop in range(far, 0, -1):
            for h in range(2):
                if hop == far and h != way:
                    continue
                sums[way, hop, h] = pltpu.make_async_remote_copy(
                    src_ref=chunk(part, slot_of(way, hop), core, h),
                    dst_ref=inbox.at[way, hop - 1, h],
                    send_sem=rs_send.at[way, hop - 1, h],
                    recv_sem=rs_recv.at[way, hop - 1, h],
                    device_id=toward[1 - way],
                    device_id_type=MESH,
                )

    def add_and_send(way, hop, h):
        slot = slot_of(way, hop)
        here = pl.ds(start_row(slot, core, h), half)
        total = part[here, :].astype(jnp.float32) + pair[slot, h * half : (h + 1) * half, :].astype(
            jnp.float32
        )
        if (way, hop + 1, h) in sums:
            sums[way, hop + 1, h].wait_recv()
            total = total + inbox[way, hop, h].astype(jnp.float32)
        part[here, :] = total.astype(jnp.bfloat16)
        sums[way, hop, h].start()

    for h in range(2):
        for way in range(2):
            at = h if way == 0 else 1 - h
            if (way, 0, at) in gathers:
                gathers[way, 0, at].start()
    shares[0].start()
    for load in loads:
        load.wait()
    own_copy.wait()
    shares[0].wait_recv()
    compute(0, 1)
    answers[0].start()
    for hop in range(1, far + 1):
        for h in range(2):
            for way in range(2):
                at = h if way == 0 else 1 - h
                if (way, hop - 1, at) in gathers:
                    gathers[way, hop - 1, at].wait_recv()
                if (way, hop, at) in gathers:
                    gathers[way, hop, at].start()
        slots = (hop, count - hop) if hop < far else (far,)
        for slot in slots:
            shares[slot].start()
        for slot in slots:
            shares[slot].wait_recv()
        compute(hop, len(slots))
        for slot in slots:
            answers[slot].start()
        if hop == far - 1:
            for way in range(2):
                answers[slot_of(way, hop)].wait_recv()
            for way in range(2):
                add_and_send(way, hop, 1 - way)

    answers[far].wait_recv()
    for way in range(2):
        add_and_send(way, far, way)
    for way in range(2):
        add_and_send(way, far - 1, way)
    for hop in range(far - 2, 0, -1):
        for way in range(2):
            answers[slot_of(way, hop)].wait_recv()
        for turn in range(2):
            for way in range(2):
                add_and_send(way, hop, 1 - way if turn == 0 else way)
    answers[0].wait_recv()
    for h in range(2):
        here = pl.ds(start_row(0, core, h), half)
        total = part[here, :].astype(jnp.float32) + pair[0, h * half : (h + 1) * half, :].astype(
            jnp.float32
        )
        for way in range(2):
            if (way, 1, h) in sums:
                sums[way, 1, h].wait_recv()
                total = total + inbox[way, 0, h].astype(jnp.float32)
        out_ref[h * half : (h + 1) * half, :] = total.astype(out_ref.dtype)
    for group in (gathers, shares, answers, sums):
        for copy in group.values():
            copy.wait_send()


def taken_bound(rows, top_count, experts):
    capacity = rows * top_count * 5 // (4 * experts)
    return -(-2 * capacity // 16) * 16


def moe_scratch(count, rows, padded, width, hidden, taken_most):
    half = rows // 2
    far = count // 2
    tall = count * 2 * rows
    bf16 = jnp.bfloat16
    return [
        ((tall, padded), bf16),
        ((tall, width), bf16),
        ((count, rows, width), bf16),
        ((2, far, 2, half, width), bf16),
        ((width, hidden), bf16),
        ((width, hidden), bf16),
        ((hidden, width), bf16),
        ((2 * taken_most, hidden), bf16),
        ((2 * taken_most, width), bf16),
    ]


def moe(rows_in, width, experts, top_count, w_gate, w_up, w_down, folded):
    count = lax.axis_size("seq")
    rows, padded = rows_in.shape
    far = count // 2
    dma = pltpu.SemaphoreType.DMA
    taken_most = taken_bound(rows, top_count, experts)
    scratch = moe_scratch(count, rows, padded, width, w_gate.shape[2], taken_most)
    tall = count * 2 * rows
    return pl.pallas_call(
        functools.partial(moe_kernel, count, folded, experts, taken_most),
        out_shape=jax.ShapeDtypeStruct((rows, width), jnp.bfloat16),
        in_specs=[pl.BlockSpec(memory_space=pltpu.VMEM)]
        + [pl.BlockSpec(memory_space=pl.ANY)] * 3,
        out_specs=pl.BlockSpec(memory_space=pltpu.VMEM),
        scratch_shapes=[pltpu.VMEM(shape, dtype) for shape, dtype in scratch]
        + [
            dma((4,)),
            dma((2, far, 2)),
            dma((2, far, 2)),
            dma((count,)),
            dma((count,)),
            dma((2, far, 2)),
            dma((2, far, 2)),
            dma((count,)),
            dma((count,)),
        ],
        compiler_params=pltpu.CompilerParams(
            collective_id=0, has_side_effects=True, vmem_limit_bytes=VMEM_MOST
        ),
        cost_estimate=pl.CostEstimate(
            flops=6 * tall * width * w_gate.shape[2],
            bytes_accessed=6 * width * w_gate.shape[2],
            transcendentals=tall * w_gate.shape[2],
        ),
    )(rows_in, w_gate, w_up, w_down)


def moe_fits(count, heads, rows, padded, width, w_gate, taken_most):
    if heads != 2 or count < 4 or count % 2 or w_gate.shape[0] != 1:
        return False
    if rows % 32 or width % TILE or w_gate.shape[2] % TILE:
        return False
    need = 0
    for shape, _ in moe_scratch(count, rows, padded, width, w_gate.shape[2], taken_most):
        size = 2
        for extent in shape:
            size *= extent
        need += size
    return need < VMEM_MOST * 7 // 8


def shards(
    folded,
    query_proj,
    key_proj,
    value_proj,
    segment_ids,
    feature_map,
    head_gain,
    residual,
    out_weight,
    norm_gain,
    router,
    w_gate,
    w_up,
    w_down,
    expert_ids,
):
    attn_heads = attention(query_proj, key_proj, value_proj, segment_ids, feature_map, head_gain)
    row_count = residual.shape[0]
    head_place = lax.axis_index("head")
    head_devs = lax.axis_size("head")
    sums = jnp.dot(attn_heads, out_weight, preferred_element_type=jnp.float32)
    projected = lax.dynamic_slice_in_dim(sums, head_place * row_count, row_count)
    for step in range(1, head_devs):
        target = (head_place + step) % head_devs
        projected = projected + lax.ppermute(
            lax.dynamic_slice_in_dim(sums, target * row_count, row_count),
            "head",
            [(i, (i + step) % head_devs) for i in range(head_devs)],
        )
    hidden = (residual.astype(jnp.float32) + projected).astype(jnp.bfloat16)
    hidden_f = hidden.astype(jnp.float32)
    normed = (
        hidden_f
        * lax.rsqrt(jnp.mean(hidden_f * hidden_f, axis=1, keepdims=True) + 1e-05)
        * norm_gain
    ).astype(jnp.bfloat16)
    logits = jnp.dot(normed, router, preferred_element_type=jnp.float32)
    expert_count = router.shape[1]
    expert_iota = lax.iota(jnp.int32, expert_count)
    picked = expert_ids[:, :, None] == expert_iota[None, None, :]
    chosen = jnp.sum(jnp.where(picked, logits[:, None, :], 0.0), axis=2)
    gates = jax.nn.sigmoid(chosen)
    gate_weights = gates / jnp.sum(gates, axis=1, keepdims=True)
    dense_gates = jnp.sum(jnp.where(picked, gate_weights[:, :, None], 0.0), axis=1)
    model_width = normed.shape[1]
    coarse = lax.reduce_precision(dense_gates, 8, 7)
    lanes = -(-2 * expert_count // 128) * 128
    extra = jnp.concatenate([coarse, dense_gates - coarse], axis=1).astype(jnp.bfloat16)
    extra = jnp.pad(extra, ((0, 0), (0, lanes - 2 * expert_count)))
    top_count = expert_ids.shape[1]
    taken_most = taken_bound(row_count, top_count, expert_count)
    if moe_fits(
        lax.axis_size("seq"), head_devs, row_count, model_width + lanes, model_width, w_gate, taken_most
    ):
        rows_in = jnp.concatenate([normed, extra], axis=1)
        expert_sum = moe(rows_in, model_width, expert_count, top_count, w_gate, w_up, w_down, folded)
        return (hidden, expert_sum)
    spread = ("seq", "head")
    all_rows = lax.all_gather(normed, spread, axis=0, tiled=True)
    all_gates = lax.all_gather(dense_gates, spread, axis=0, tiled=True)
    exp_dev = w_gate.shape[0]
    first = (lax.axis_index("seq") * lax.axis_size("head") + lax.axis_index("head")) * exp_dev
    partial = 0.0
    for own in range(exp_dev):
        gate = jnp.sum(jnp.where(expert_iota[None, :] == first + own, all_gates, 0.0), axis=1)
        partial = partial + run_expert(all_rows, gate, w_gate[own], w_up[own], w_down[own])
    expert_sum = lax.psum_scatter(
        partial.astype(jnp.bfloat16), spread, scatter_dimension=0, tiled=True
    )
    return (hidden, expert_sum)


def folded_seq(mesh):
    chips = [getattr(d, "coords", None) for d in mesh.devices[0, :3, 0]]
    if None in chips or len(chips) < 3:
        return True
    moved = [sum(abs(i - j) for i, j in zip(a, b)) for a, b in zip(chips, chips[1:])]
    return moved[0] == 1 and moved[1] == 2


def solution(mesh):
    placed = (
        P(("groups", "seq"), "head"),
        P(("groups", "seq"), "head"),
        P(("groups", "seq"), "head"),
        P(("groups", "seq")),
        P("head", None, None),
        P("head"),
        P(("groups", "seq", "head"), None),
        P("head", None),
        P(),
        P(),
        P(("seq", "head"), None, None),
        P(("seq", "head"), None, None),
        P(("seq", "head"), None, None),
        P(("groups", "seq", "head"), None),
    )
    return jax.shard_map(
        functools.partial(shards, folded_seq(mesh)),
        mesh=mesh,
        in_specs=placed,
        out_specs=(P(("groups", "seq", "head"), None), P(("groups", "seq", "head"), None)),
        check_vma=False,
    )
```

```python
import functools

import jax
import jax.numpy as jnp
from jax import lax
from jax.experimental import pallas as pl
from jax.experimental.pallas import tpu as pltpu
from jax.sharding import PartitionSpec as P


def run_expert(rows, gate, w_gate, w_up, w_down):
    gate_pre = jnp.dot(rows, w_gate, preferred_element_type=jnp.float32)
    up_pre = jnp.dot(rows, w_up, preferred_element_type=jnp.float32)
    activated = (jax.nn.silu(gate_pre) * up_pre).astype(jnp.bfloat16)
    answer = jnp.dot(activated, w_down, preferred_element_type=jnp.float32)
    return answer * gate[:, None]


MESH = pl.DeviceIdType.MESH


def spans_of(token_count, blocks):
    longest = token_count * blocks // 3
    reach = min(blocks - 1, max(1, (longest - 2) // token_count + 1))
    spans = []
    while sum(spans) < reach:
        spans.append(2 ** len(spans))
    return spans


def attn_kernel(
    blocks,
    spans,
    q_hbm,
    k_hbm,
    v_hbm,
    seg_col,
    seg_row,
    map_hbm,
    gain_ref,
    out_ref,
    q_ref,
    k_ref,
    v_ref,
    map_ref,
    load_sem,
    key_feat,
    query_feat,
    window,
    carried,
    within,
    outbox,
    inbox,
    seg_out,
    seg_in,
    send_sem,
    recv_sem,
    seg_send,
    seg_recv,
):
    tokens = q_ref.shape[0]
    heads, dim, _ = map_ref.shape
    place = lax.axis_index("seq")
    f32, bf16 = jnp.float32, jnp.bfloat16

    sources = ((k_hbm, k_ref), (map_hbm, map_ref), (v_hbm, v_ref), (q_hbm, q_ref))
    loads = [
        pltpu.make_async_copy(src, dst, load_sem.at[i]) for i, (src, dst) in enumerate(sources)
    ]
    for load in loads:
        load.start()

    barrier = pltpu.get_barrier_semaphore()
    for span in spans:
        for shift in (span, blocks - span):
            other = (place + shift) % blocks
            pl.semaphore_signal(barrier, inc=1, device_id={"seq": other}, device_id_type=MESH)
    pl.semaphore_wait(barrier, 2 * len(spans))

    def packet(i, h):
        return pltpu.make_async_remote_copy(
            src_ref=outbox.at[i, h],
            dst_ref=inbox.at[i, h],
            send_sem=send_sem.at[i, h],
            recv_sem=recv_sem.at[i, h],
            device_id={"seq": place + spans[i]},
            device_id_type=MESH,
        )

    def note(i):
        return pltpu.make_async_remote_copy(
            src_ref=seg_out,
            dst_ref=seg_in.at[i],
            send_sem=seg_send.at[i],
            recv_sem=seg_recv.at[i],
            device_id={"seq": place + spans[i]},
            device_id_type=MESH,
        )

    last = seg_col[tokens - 1 : tokens, :]
    seg_out[...] = jnp.broadcast_to(last.astype(f32), seg_out.shape)
    for i, span in enumerate(spans):

        @pl.when(place + span < blocks)
        def _tell(i=i):
            note(i).start()

        @pl.when(place < span)
        def _none(i=i):
            seg_in[i] = jnp.full(seg_in.shape[1:], -1.0, f32)
            inbox[i] = jnp.zeros(inbox.shape[1:], bf16)

    def features(x, h):
        projected = jnp.dot(x, map_ref[h], preferred_element_type=f32)
        return jnp.where(projected > 0, projected + 1.0, jnp.exp(jnp.minimum(projected, 0.0))).astype(
            bf16
        )

    def lanes(h):
        return pl.ds(pl.multiple_of(h * dim, dim), dim)

    def send(i, h):
        outbox[i, h] = window[h].astype(bf16)

        @pl.when(place + spans[i] < blocks)
        def _go():
            packet(i, h).start()

    tail = seg_col[...] == last

    def key_step(h, carry):
        feat = features(k_ref[:, lanes(h)], h)
        key_feat[h] = feat
        tail_values = jnp.where(tail, v_ref[:, lanes(h)].astype(f32), 0.0).astype(bf16)
        window[h] = lax.dot_general(
            feat, tail_values, (((0,), (0,)), ((), ())), preferred_element_type=f32
        )
        send(0, h)
        return carry

    for load in loads[:3]:
        load.wait()
    lax.fori_loop(0, heads, key_step, 0)
    loads[3].wait()
    for i, span in enumerate(spans):

        @pl.when(place >= span)
        def _told(i=i):
            note(i).wait_recv()

    last_f = last.astype(f32)
    before = seg_in[0, 0:1, 0:1]
    reached = seg_col[...].astype(f32) == before
    row = lax.broadcasted_iota(jnp.int32, (tokens, tokens), 0)
    col = lax.broadcasted_iota(jnp.int32, (tokens, tokens), 1)
    allowed = (col <= row) & (seg_col[...] == seg_row[...])

    def take(i, h):
        @pl.when(place >= spans[i])
        def _arrived():
            packet(i, h).wait_recv()

        shifted = inbox[i, h].astype(f32)
        seg = seg_in[i, 0:1, 0:1]
        if i == 0:
            carried[h] = shifted
        else:
            carried[h] = carried[h] + jnp.where(seg == before, shifted, 0.0)
        if i + 1 < len(spans):
            window[h] = window[h] + jnp.where(seg == last_f, shifted, 0.0)
            send(i + 1, h)

    def finish(h):
        far = jnp.dot(query_feat[h], carried[h].astype(bf16), preferred_element_type=f32)
        mixed = within[:, lanes(h)] + jnp.where(reached, far, 0.0)
        scale = lax.rsqrt(jnp.mean(mixed * mixed, axis=1, keepdims=True) + 1e-06)
        out_ref[:, lanes(h)] = (mixed * scale * gain_ref[:, lanes(h)]).astype(bf16)

    def query_step(h, carry):
        feat = features(q_ref[:, lanes(h)], h)
        query_feat[h] = feat
        scores = lax.dot_general(
            feat, key_feat[h], (((1,), (1,)), ((), ())), preferred_element_type=f32
        )
        weights = jnp.where(allowed, scores, 0.0).astype(bf16)
        within[:, lanes(h)] = jnp.dot(weights, v_ref[:, lanes(h)], preferred_element_type=f32)
        take(0, h)
        return carry

    lax.fori_loop(0, heads, query_step, 0)
    for i in range(1, len(spans)):

        def later_step(h, carry, i=i):
            take(i, h)
            if i == len(spans) - 1:
                finish(h)
            return carry

        lax.fori_loop(0, heads, later_step, 0)
    if len(spans) == 1:

        def last_step(h, carry):
            finish(h)
            return carry

        lax.fori_loop(0, heads, last_step, 0)

    for i, span in enumerate(spans):

        @pl.when(place + span < blocks)
        def _sent(i=i):
            note(i).wait_send()

            def done_step(h, carry):
                packet(i, h).wait_send()
                return carry

            lax.fori_loop(0, heads, done_step, 0)


def attention(query_proj, key_proj, value_proj, segment_ids, feature_map, head_gain):
    tokens = query_proj.shape[0]
    heads, dim, feat = feature_map.shape
    blocks = lax.axis_size("seq")
    spans = spans_of(tokens, blocks)
    count = len(spans)
    dma = pltpu.SemaphoreType.DMA
    f32, bf16 = jnp.float32, jnp.bfloat16
    in_any = pl.BlockSpec(memory_space=pl.ANY)
    in_vmem = pl.BlockSpec(memory_space=pltpu.VMEM)
    return pl.pallas_call(
        functools.partial(attn_kernel, blocks, spans),
        out_shape=jax.ShapeDtypeStruct((tokens, heads * dim), bf16),
        in_specs=[in_any, in_any, in_any, in_vmem, in_vmem, in_any, in_vmem],
        out_specs=pl.BlockSpec(memory_space=pltpu.VMEM),
        scratch_shapes=[
            pltpu.VMEM(query_proj.shape, bf16),
            pltpu.VMEM(key_proj.shape, bf16),
            pltpu.VMEM(value_proj.shape, bf16),
            pltpu.VMEM(feature_map.shape, bf16),
            dma((4,)),
            pltpu.VMEM((heads, tokens, feat), bf16),
            pltpu.VMEM((heads, tokens, feat), bf16),
            pltpu.VMEM((heads, feat, dim), f32),
            pltpu.VMEM((heads, feat, dim), f32),
            pltpu.VMEM((tokens, heads * dim), f32),
            pltpu.VMEM((count, heads, feat, dim), bf16),
            pltpu.VMEM((count, heads, feat, dim), bf16),
            pltpu.VMEM((8, 128), f32),
            pltpu.VMEM((count, 8, 128), f32),
            dma((count, heads)),
            dma((count, heads)),
            dma((count,)),
            dma((count,)),
        ],
        compiler_params=pltpu.CompilerParams(
            collective_id=1, has_side_effects=True, vmem_limit_bytes=VMEM_MOST
        ),
    )(
        query_proj,
        key_proj,
        value_proj,
        segment_ids.reshape(tokens, 1),
        segment_ids.reshape(1, tokens),
        feature_map,
        head_gain.reshape(1, heads * dim),
    )


TILE = 1024
VMEM_MOST = 63 * 1024 * 1024


def ring_place(index, count, folded):
    if not folded:
        return index
    far, side = index // 2, index % 2
    return far + side * (count - 1 - 2 * far)


def ring_index(place, count, folded):
    if not folded:
        return place
    side = place // (count // 2)
    far = place + side * (count - 1 - 2 * place)
    return 2 * far + side


def moe_kernel(
    count,
    folded,
    experts,
    x_ref,
    wg_hbm,
    wu_hbm,
    wd_hbm,
    out_ref,
    rows_buf,
    part,
    pair,
    inbox,
    wg,
    wu,
    wd,
    act,
    load_sem,
    ag_send,
    ag_recv,
    sib_send,
    sib_recv,
    rs_send,
    rs_recv,
    pair_send,
    pair_recv,
):
    rows, padded = x_ref.shape
    width = out_ref.shape[1]
    half = rows // 2
    far = count // 2
    core = lax.axis_index("head")
    seq = lax.axis_index("seq")
    place = ring_place(seq, count, folded)
    ahead = {"seq": ring_index((place + 1) % count, count, folded)}
    behind = {"seq": ring_index((place + count - 1) % count, count, folded)}
    sibling = {"head": 1 - core}
    toward = (ahead, behind)

    loads = [
        pltpu.make_async_copy(src.at[0], dst, load_sem.at[i])
        for i, (src, dst) in enumerate(((wg_hbm, wg), (wu_hbm, wu), (wd_hbm, wd)))
    ]
    for load in loads:
        load.start()

    barrier = pltpu.get_barrier_semaphore()
    for other in (ahead, behind, sibling):
        pl.semaphore_signal(barrier, inc=1, device_id=other, device_id_type=MESH)
    pl.semaphore_wait(barrier, 3)

    def spot(slot):
        if slot == 0:
            return 0
        if slot == far:
            return count - 1
        return 2 * slot - 1 if slot < far else 2 * (count - slot)

    def start_row(slot, which, part_of=0):
        return pl.multiple_of((spot(slot) * 2 + which) * rows + part_of * half, half)

    def block(ref, slot, which):
        return ref.at[pl.ds(start_row(slot, which), rows)]

    def chunk(ref, slot, which, h):
        return ref.at[pl.ds(start_row(slot, which, h), half)]

    def slot_of(way, hop):
        return hop if way == 0 else (count - hop) % count

    own_copy = pltpu.make_async_copy(x_ref, block(rows_buf, 0, core), load_sem.at[3])
    own_copy.start()

    gathers = {}
    for way in range(2):
        for hop in range(far):
            for h in range(2):
                if hop == far - 1 and h != way:
                    continue
                if hop == 0:
                    src = x_ref.at[pl.ds(h * half, half)]
                else:
                    src = chunk(rows_buf, slot_of(way, hop), core, h)
                gathers[way, hop, h] = pltpu.make_async_remote_copy(
                    src_ref=src,
                    dst_ref=chunk(rows_buf, slot_of(way, hop + 1), core, h),
                    send_sem=ag_send.at[way, hop, h],
                    recv_sem=ag_recv.at[way, hop, h],
                    device_id=toward[way],
                    device_id_type=MESH,
                )

    shares = {}
    answers = {}
    for slot in range(count):
        src = x_ref if slot == 0 else block(rows_buf, slot, core)
        shares[slot] = pltpu.make_async_remote_copy(
            src_ref=src,
            dst_ref=block(rows_buf, slot, core),
            send_sem=sib_send.at[slot],
            recv_sem=sib_recv.at[slot],
            device_id=sibling,
            device_id_type=MESH,
        )
        answers[slot] = pltpu.make_async_remote_copy(
            src_ref=block(part, slot, 1 - core),
            dst_ref=pair.at[slot],
            send_sem=pair_send.at[slot],
            recv_sem=pair_recv.at[slot],
            device_id=sibling,
            device_id_type=MESH,
        )

    def compute(first_slot, blocks):
        low = spot(first_slot) * 2 * rows
        tall = blocks * 2 * rows
        expert = lax.axis_index("seq") * 2 + core
        taken = pl.ds(low, tall)
        extra = rows_buf[taken, width:].astype(jnp.float32)
        lane = lax.broadcasted_iota(jnp.int32, extra.shape, 1)
        mine = (lane == expert) | (lane == expert + experts)
        gate = jnp.sum(jnp.where(mine, extra, 0.0), axis=1, keepdims=True)

        def up_step(t, carry):
            cols = pl.ds(pl.multiple_of(t * TILE, TILE), TILE)
            x = rows_buf[taken, :width]
            gate_pre = jnp.dot(x, wg[:, cols], preferred_element_type=jnp.float32)
            up_pre = jnp.dot(x, wu[:, cols], preferred_element_type=jnp.float32)
            act[:tall, cols] = (gate_pre * jax.nn.sigmoid(gate_pre) * up_pre).astype(jnp.bfloat16)
            return carry

        lax.fori_loop(0, wg.shape[1] // TILE, up_step, 0)

        def down_step(t, carry):
            cols = pl.ds(pl.multiple_of(t * TILE, TILE), TILE)
            answer = jnp.dot(act[:tall, :], wd[:, cols], preferred_element_type=jnp.float32)
            part[taken, cols] = (answer * gate).astype(jnp.bfloat16)
            return carry

        lax.fori_loop(0, width // TILE, down_step, 0)

    sums = {}
    for way in range(2):
        for hop in range(far, 0, -1):
            for h in range(2):
                if hop == far and h != way:
                    continue
                sums[way, hop, h] = pltpu.make_async_remote_copy(
                    src_ref=chunk(part, slot_of(way, hop), core, h),
                    dst_ref=inbox.at[way, hop - 1, h],
                    send_sem=rs_send.at[way, hop - 1, h],
                    recv_sem=rs_recv.at[way, hop - 1, h],
                    device_id=toward[1 - way],
                    device_id_type=MESH,
                )

    def add_and_send(way, hop, h):
        slot = slot_of(way, hop)
        here = pl.ds(start_row(slot, core, h), half)
        total = part[here, :].astype(jnp.float32) + pair[slot, h * half : (h + 1) * half, :].astype(
            jnp.float32
        )
        if (way, hop + 1, h) in sums:
            sums[way, hop + 1, h].wait_recv()
            total = total + inbox[way, hop, h].astype(jnp.float32)
        part[here, :] = total.astype(jnp.bfloat16)
        sums[way, hop, h].start()

    for h in range(2):
        for way in range(2):
            at = h if way == 0 else 1 - h
            if (way, 0, at) in gathers:
                gathers[way, 0, at].start()
    shares[0].start()
    for load in loads:
        load.wait()
    own_copy.wait()
    shares[0].wait_recv()
    compute(0, 1)
    answers[0].start()
    for hop in range(1, far + 1):
        for h in range(2):
            for way in range(2):
                at = h if way == 0 else 1 - h
                if (way, hop - 1, at) in gathers:
                    gathers[way, hop - 1, at].wait_recv()
                if (way, hop, at) in gathers:
                    gathers[way, hop, at].start()
        slots = (hop, count - hop) if hop < far else (far,)
        for slot in slots:
            shares[slot].start()
        for slot in slots:
            shares[slot].wait_recv()
        compute(hop, len(slots))
        for slot in slots:
            answers[slot].start()
        if hop == far - 1:
            for way in range(2):
                answers[slot_of(way, hop)].wait_recv()
            for way in range(2):
                add_and_send(way, hop, 1 - way)

    answers[far].wait_recv()
    for way in range(2):
        add_and_send(way, far, way)
    for way in range(2):
        add_and_send(way, far - 1, way)
    for hop in range(far - 2, 0, -1):
        for way in range(2):
            answers[slot_of(way, hop)].wait_recv()
        for turn in range(2):
            for way in range(2):
                add_and_send(way, hop, 1 - way if turn == 0 else way)
    answers[0].wait_recv()
    for h in range(2):
        here = pl.ds(start_row(0, core, h), half)
        total = part[here, :].astype(jnp.float32) + pair[0, h * half : (h + 1) * half, :].astype(
            jnp.float32
        )
        for way in range(2):
            if (way, 1, h) in sums:
                sums[way, 1, h].wait_recv()
                total = total + inbox[way, 0, h].astype(jnp.float32)
        out_ref[h * half : (h + 1) * half, :] = total.astype(out_ref.dtype)
    for group in (gathers, shares, answers, sums):
        for copy in group.values():
            copy.wait_send()


def moe_scratch(count, rows, padded, width, hidden):
    half = rows // 2
    far = count // 2
    tall = count * 2 * rows
    bf16 = jnp.bfloat16
    return [
        ((tall, padded), bf16),
        ((tall, width), bf16),
        ((count, rows, width), bf16),
        ((2, far, 2, half, width), bf16),
        ((width, hidden), bf16),
        ((width, hidden), bf16),
        ((hidden, width), bf16),
        ((4 * rows, hidden), bf16),
    ]


def moe(rows_in, width, experts, w_gate, w_up, w_down, folded):
    count = lax.axis_size("seq")
    rows, padded = rows_in.shape
    far = count // 2
    dma = pltpu.SemaphoreType.DMA
    scratch = moe_scratch(count, rows, padded, width, w_gate.shape[2])
    tall = count * 2 * rows
    return pl.pallas_call(
        functools.partial(moe_kernel, count, folded, experts),
        out_shape=jax.ShapeDtypeStruct((rows, width), jnp.bfloat16),
        in_specs=[pl.BlockSpec(memory_space=pltpu.VMEM)]
        + [pl.BlockSpec(memory_space=pl.ANY)] * 3,
        out_specs=pl.BlockSpec(memory_space=pltpu.VMEM),
        scratch_shapes=[pltpu.VMEM(shape, dtype) for shape, dtype in scratch]
        + [
            dma((4,)),
            dma((2, far, 2)),
            dma((2, far, 2)),
            dma((count,)),
            dma((count,)),
            dma((2, far, 2)),
            dma((2, far, 2)),
            dma((count,)),
            dma((count,)),
        ],
        compiler_params=pltpu.CompilerParams(
            collective_id=0, has_side_effects=True, vmem_limit_bytes=VMEM_MOST
        ),
        cost_estimate=pl.CostEstimate(
            flops=6 * tall * width * w_gate.shape[2],
            bytes_accessed=6 * width * w_gate.shape[2],
            transcendentals=tall * w_gate.shape[2],
        ),
    )(rows_in, w_gate, w_up, w_down)


def moe_fits(count, heads, rows, padded, width, w_gate):
    if heads != 2 or count < 4 or count % 2 or w_gate.shape[0] != 1:
        return False
    if rows % 32 or width % TILE or w_gate.shape[2] % TILE:
        return False
    need = 0
    for shape, _ in moe_scratch(count, rows, padded, width, w_gate.shape[2]):
        size = 2
        for extent in shape:
            size *= extent
        need += size
    return need < VMEM_MOST * 7 // 8


def shards(
    folded,
    query_proj,
    key_proj,
    value_proj,
    segment_ids,
    feature_map,
    head_gain,
    residual,
    out_weight,
    norm_gain,
    router,
    w_gate,
    w_up,
    w_down,
    expert_ids,
):
    attn_heads = attention(query_proj, key_proj, value_proj, segment_ids, feature_map, head_gain)
    row_count = residual.shape[0]
    head_place = lax.axis_index("head")
    head_devs = lax.axis_size("head")
    sums = jnp.dot(attn_heads, out_weight, preferred_element_type=jnp.float32)
    projected = lax.dynamic_slice_in_dim(sums, head_place * row_count, row_count)
    for step in range(1, head_devs):
        target = (head_place + step) % head_devs
        projected = projected + lax.ppermute(
            lax.dynamic_slice_in_dim(sums, target * row_count, row_count),
            "head",
            [(i, (i + step) % head_devs) for i in range(head_devs)],
        )
    hidden = (residual.astype(jnp.float32) + projected).astype(jnp.bfloat16)
    hidden_f = hidden.astype(jnp.float32)
    normed = (
        hidden_f
        * lax.rsqrt(jnp.mean(hidden_f * hidden_f, axis=1, keepdims=True) + 1e-05)
        * norm_gain
    ).astype(jnp.bfloat16)
    logits = jnp.dot(normed, router, preferred_element_type=jnp.float32)
    expert_count = router.shape[1]
    expert_iota = lax.iota(jnp.int32, expert_count)
    picked = expert_ids[:, :, None] == expert_iota[None, None, :]
    chosen = jnp.sum(jnp.where(picked, logits[:, None, :], 0.0), axis=2)
    gates = jax.nn.sigmoid(chosen)
    gate_weights = gates / jnp.sum(gates, axis=1, keepdims=True)
    dense_gates = jnp.sum(jnp.where(picked, gate_weights[:, :, None], 0.0), axis=1)
    model_width = normed.shape[1]
    coarse = lax.reduce_precision(dense_gates, 8, 7)
    lanes = -(-2 * expert_count // 128) * 128
    extra = jnp.concatenate([coarse, dense_gates - coarse], axis=1).astype(jnp.bfloat16)
    extra = jnp.pad(extra, ((0, 0), (0, lanes - 2 * expert_count)))
    if moe_fits(lax.axis_size("seq"), head_devs, row_count, model_width + lanes, model_width, w_gate):
        rows_in = jnp.concatenate([normed, extra], axis=1)
        expert_sum = moe(rows_in, model_width, expert_count, w_gate, w_up, w_down, folded)
        return (hidden, expert_sum)
    spread = ("seq", "head")
    all_rows = lax.all_gather(normed, spread, axis=0, tiled=True)
    all_gates = lax.all_gather(dense_gates, spread, axis=0, tiled=True)
    exp_dev = w_gate.shape[0]
    first = (lax.axis_index("seq") * lax.axis_size("head") + lax.axis_index("head")) * exp_dev
    partial = 0.0
    for own in range(exp_dev):
        gate = jnp.sum(jnp.where(expert_iota[None, :] == first + own, all_gates, 0.0), axis=1)
        partial = partial + run_expert(all_rows, gate, w_gate[own], w_up[own], w_down[own])
    expert_sum = lax.psum_scatter(
        partial.astype(jnp.bfloat16), spread, scatter_dimension=0, tiled=True
    )
    return (hidden, expert_sum)


def folded_seq(mesh):
    chips = [getattr(d, "coords", None) for d in mesh.devices[0, :3, 0]]
    if None in chips or len(chips) < 3:
        return True
    moved = [sum(abs(i - j) for i, j in zip(a, b)) for a, b in zip(chips, chips[1:])]
    return moved[0] == 1 and moved[1] == 2


def solution(mesh):
    placed = (
        P(("groups", "seq"), "head"),
        P(("groups", "seq"), "head"),
        P(("groups", "seq"), "head"),
        P(("groups", "seq")),
        P("head", None, None),
        P("head"),
        P(("groups", "seq", "head"), None),
        P("head", None),
        P(),
        P(),
        P(("seq", "head"), None, None),
        P(("seq", "head"), None, None),
        P(("seq", "head"), None, None),
        P(("groups", "seq", "head"), None),
    )
    return jax.shard_map(
        functools.partial(shards, folded_seq(mesh)),
        mesh=mesh,
        in_specs=placed,
        out_specs=(P(("groups", "seq", "head"), None), P(("groups", "seq", "head"), None)),
        check_vma=False,
    )
```
